32 devices in a mesh: groups: 2 (over x), tr: 16 (over z, y, core).
Axes of the slice: x: 2, y: 2, z: 4, core: 2. Of those that a mesh axis runs over, the one named last changes fastest.
Arguments:
- object_field: float32 [2, 16384, 1024], P(None, ('groups', 'tr')), parts along dimension 1, may hold values from -6 to 6
- probe_modes: float32 [2, 2, 256, 256], replicated, may hold values from -96 to 96
- scan_offsets: int32 [32, 8, 2], P(('groups', 'tr')), parts along dimension 0, may hold values from 0 to 768, as said below
- scan_counts: int32 [32], P(('groups', 'tr')), parts along dimension 0, may hold values from 1 to 8, as said below
- measured: int32 [32, 8, 256, 256], P(('groups', 'tr')), parts along dimension 0, may hold values from 0 to 4096
Outputs:
- object_grad: float32 [2, 16384, 1024], P(None, ('groups', 'tr')), parts along dimension 1
- probe_grad: float32 [2048, 256], P(('groups', 'tr')), parts along dimension 0
The draws below stay inside these ranges and needn't reach their ends.
There are 2 independent parts, one for each index of `groups`. The reference program is written for one: setup_inputs(seed, part) draws one part's arguments, and reference() takes and returns one part's arrays. A program takes and returns all parts, laid end to end along the dimension named above; an argument that names none is the same for every part. Nothing has to cross between parts.
Inputs may be any that keep to these rules, and one draw needn't show every extreme that they name: `scan_counts`: each tile has 1 to 8 used scan positions, and some tile has exactly 8. `scan_offsets`: row offsets lie in 0 to 511 within the tile, column offsets in 0 to 768; both ends are reached; every slot holds a valid offset, used or not.
All inputs are finite; a program needn't handle non-finite values.
Results may differ from the reference program's by a relative error of at most 0.0095.
Values may be sent and summed in bfloat16 or wider, within the bound.
No kernel may reach another device: no remote copies, remote signals or barrier semaphores. Data moves between devices by JAX's collectives and lax.ppermute only.
A program may use at most 64 MiB of HBM per device.

```python
import jax
import jax.numpy as jnp
from jax import lax

PATCH = 256
MODES = 2
ROWS = 512
COLS = 1024
PEAK_PATCH_PROBES = 8
SPECIMEN_PIECES = 16
NROWS = 8192


def draw_scan_counts(key, part):
    typical_random_seed, crowded_random_seed, picking_random_seed = jax.random.split(jax.random.fold_in(key, 11), 3)
    typical_position_tally = jax.random.randint(typical_random_seed, (SPECIMEN_PIECES,), 1, 4)
    crowded_position_draw = jax.random.randint(crowded_random_seed, (SPECIMEN_PIECES,), 0, 8)
    chosen = jax.random.randint(picking_random_seed, (), 0, SPECIMEN_PIECES)
    tile_ids = jnp.arange(SPECIMEN_PIECES)
    filled_places = jnp.where(crowded_position_draw == 0, PEAK_PATCH_PROBES, typical_position_tally)
    return jnp.where(tile_ids == chosen, PEAK_PATCH_PROBES, filled_places).astype(jnp.int32)


def draw_scan_offsets(key, part):
    key_rows, key_cols, key_high, key_low = jax.random.split(jax.random.fold_in(key, 23), 4)
    row_offset = jax.random.randint(key_rows, (SPECIMEN_PIECES, PEAK_PATCH_PROBES), 0, ROWS)
    col_offset = jax.random.randint(key_cols, (SPECIMEN_PIECES, PEAK_PATCH_PROBES), 0, COLS - PATCH + 1)
    pick_high = jax.random.randint(key_high, (), 0, SPECIMEN_PIECES)
    pick_low = jax.random.randint(key_low, (), 0, SPECIMEN_PIECES)
    tile_ids = jnp.arange(SPECIMEN_PIECES)[:, None]
    slot_ids = jnp.arange(PEAK_PATCH_PROBES)[None, :]
    high_spot = (tile_ids == pick_high) & (slot_ids == 0)
    low_spot = (tile_ids == pick_low) & (slot_ids == 1)
    row_offset = jnp.where(high_spot, ROWS - 1, jnp.where(low_spot, 0, row_offset))
    col_offset = jnp.where(high_spot, COLS - PATCH, jnp.where(low_spot, 0, col_offset))
    return jnp.stack([row_offset, col_offset], axis=-1).astype(jnp.int32)


def place_ends(drawn, key, low, largest):
    shape = drawn.shape
    index_at = [jax.random.randint(jax.random.fold_in(key, axis), (), 0, shape[axis]) for axis in range(len(shape))]
    drawn = drawn.at[tuple(index_at)].set(low)
    longest = shape.index(max(shape))
    index_at[longest] = (index_at[longest] + 1) % shape[longest]
    return drawn.at[tuple(index_at)].set(largest)


def block_levels(stream_key, extent, cuts, least, high):
    loudness = 1.0
    for position, shards_of in cuts:
        steps = jax.random.uniform(jax.random.fold_in(jax.random.fold_in(stream_key, 6), position), (shards_of,), jnp.float32, least / len(cuts), high / len(cuts))
        loudness = loudness * jnp.repeat(jnp.exp(steps), extent[position] // shards_of).reshape((-1,) + (1,) * (len(extent) - 1 - position))
    return loudness


def centred(stream_key, shape, deviation, most, shards=(), kind=jnp.bfloat16):
    entries = jax.random.normal(stream_key, shape, jnp.float32) * deviation
    if len(shards) > 0:
        entries = block_levels(stream_key, shape, shards, -0.22, 0.18) * entries
    return jnp.clip(entries, min=-most, max=most).astype(kind)


def setup_inputs(seed: int = 0, part: int = 0) -> dict:
    splits = jax.random.split(jax.random.key(seed), 6)
    part_keys = jax.random.split(jax.random.fold_in(splits[5], part), 6)
    object_field = centred(part_keys[0], (2, NROWS, COLS), 1.0, 6.0, ((1, 16),), jnp.float32)
    probe_modes = centred(splits[1], (MODES, 2, PATCH, PATCH), 16.0, 96.0, (), jnp.float32)
    scan_offsets = draw_scan_offsets(jax.random.fold_in(jax.random.fold_in(splits[5], part), 71), part)
    scan_counts = draw_scan_counts(jax.random.fold_in(jax.random.fold_in(splits[5], part), 71), part)
    measured = place_ends(jax.random.randint(part_keys[4], (SPECIMEN_PIECES, PEAK_PATCH_PROBES, PATCH, PATCH), 0, 4097), jax.random.fold_in(part_keys[4], 1), 0, 4096).astype(jnp.int32)
    return dict(object_field=object_field, probe_modes=probe_modes, scan_offsets=scan_offsets, scan_counts=scan_counts, measured=measured)


loss_scale = 1.0 / 1024.0

def dft_table(patch_size):
    index_run = jnp.arange(patch_size, dtype=jnp.int32)
    product = index_run[:, None] * index_run[None, :] % patch_size
    phase_angle = -2.0 * jnp.pi / patch_size * product.astype(jnp.float32)
    unit_scale = 1.0 / jnp.sqrt(jnp.float32(patch_size))
    table_real = jnp.cos(phase_angle) * unit_scale
    table_imag = jnp.sin(phase_angle) * unit_scale
    upper_rows = jnp.concatenate([table_real, table_imag], axis=1)
    lower_rows = jnp.concatenate([-table_imag, table_real], axis=1)
    return jnp.concatenate([upper_rows, lower_rows], axis=0).astype(jnp.bfloat16)

def matmul_exact(form, left_side, right_side):
    return jnp.einsum(form, left_side.astype(jnp.float32), right_side.astype(jnp.float32), precision=lax.Precision.HIGHEST)

def patch_grads(patch, sqrt_counts, probe_modes, dft_matrix):
    patch_size = patch.shape[-1]
    mode_count = probe_modes.shape[0]
    probe_real = probe_modes[:, 0]
    probe_imag = probe_modes[:, 1]
    object_real = patch[0]
    object_imag = patch[1]
    exit_real = probe_real * object_real - probe_imag * object_imag
    exit_imag = probe_real * object_imag + probe_imag * object_real
    exit_wave = jnp.concatenate([exit_real, exit_imag], axis=-1).astype(jnp.bfloat16)
    half_done = matmul_exact('mpk,kl->mpl', exit_wave, dft_matrix).astype(jnp.bfloat16)
    stacked = jnp.concatenate([half_done[..., :patch_size], half_done[..., patch_size:]], axis=1)
    far_field = matmul_exact('kq,mkp->mqp', dft_matrix, stacked)
    far_real = far_field[:, :patch_size]
    far_imag = far_field[:, patch_size:]
    model_power = lax.optimization_barrier(jnp.sum(far_real * far_real + far_imag * far_imag, axis=0))
    factor = 2.0 * loss_scale * (1.0 - sqrt_counts / jnp.sqrt(model_power + 1.0))
    grad_far = (far_field.reshape(mode_count, 2, patch_size, patch_size) * factor).reshape(mode_count, 2 * patch_size, patch_size).astype(jnp.bfloat16)
    back_rows = matmul_exact('qk,mkp->mqp', dft_matrix, grad_far).astype(jnp.bfloat16)
    col_major = jnp.concatenate([back_rows[:, :patch_size], back_rows[:, patch_size:]], axis=-1)
    grad_wave = matmul_exact('mpk,lk->mpl', col_major, dft_matrix)
    grad_real = grad_wave[..., :patch_size]
    grad_imag = grad_wave[..., patch_size:]
    obj_real = lax.optimization_barrier(jnp.sum(probe_real * grad_real + probe_imag * grad_imag, axis=0))
    obj_imag = lax.optimization_barrier(jnp.sum(probe_real * grad_imag - probe_imag * grad_real, axis=0))
    probe_greal = object_real * grad_real + object_imag * grad_imag
    probe_gimag = object_real * grad_imag - object_imag * grad_real
    return (jnp.stack([obj_real, obj_imag]), jnp.stack([probe_greal, probe_gimag], axis=1))

def reference(object_field, probe_modes, scan_offsets, scan_counts, measured):
    extended = jnp.concatenate([object_field, jnp.zeros((2, PATCH, COLS), jnp.float32)], axis=1)
    sqrt_counts = jnp.sqrt(measured.astype(jnp.float32))
    dft_matrix = dft_table(PATCH)

    def tile_loop(tile_index, loop_state):

        def slot_loop(slot_index, inner_state):
            gradient, probe_sum = inner_state
            row_start = (tile_index * ROWS + scan_offsets[tile_index, slot_index, 0]).astype(jnp.int32)
            col_start = scan_offsets[tile_index, slot_index, 1].astype(jnp.int32)
            corner = (jnp.int32(0), row_start, col_start)
            patch = lax.dynamic_slice(extended, corner, (2, PATCH, PATCH))
            part_object, part_probe = patch_grads(patch, sqrt_counts[tile_index, slot_index], probe_modes, dft_matrix)
            current = lax.dynamic_slice(gradient, corner, (2, PATCH, PATCH))
            gradient = lax.dynamic_update_slice(gradient, current + part_object, corner)
            return (gradient, probe_sum + part_probe)
        return lax.fori_loop(jnp.int32(0), scan_counts[tile_index], slot_loop, loop_state)
    start_state = (jnp.zeros((2, NROWS + PATCH, COLS), jnp.float32), jnp.zeros((MODES, 2, PATCH, PATCH), jnp.float32))
    gradient, probe_sum = lax.fori_loop(jnp.int32(0), jnp.int32(SPECIMEN_PIECES), tile_loop, start_state)
    return (gradient[:, :NROWS, :], probe_sum.reshape(2 * MODES * PATCH, PATCH))
```

```python
import functools

import jax
import jax.numpy as jnp
import ml_dtypes
import numpy as np
from jax import lax
from jax.experimental import pallas as pl
from jax.experimental.pallas import tpu as pltpu
from jax.sharding import PartitionSpec as P

loss_scale = 1.0 / 1024.0
LANES = 128


def shifted(value, axis, steps):
    count = lax.axis_size(axis)
    initial, last = (max(0, -steps), min(count, count - steps))
    return lax.ppermute(value, axis, [(source, source + steps) for source in range(initial, last)])


def dft_tables(size):
    index = np.arange(size)
    angle = -2.0 * np.pi / size * (index[:, None] * index[None, :] % size)
    scale = 1.0 / np.sqrt(size)
    real = np.cos(angle) * scale
    imag = np.sin(angle) * scale
    table = np.block([[real, imag], [-imag, real]]).astype(np.float32)
    table = table.astype(ml_dtypes.bfloat16)
    return table, np.ascontiguousarray(table.T)


def one_slot(row, col, obj, acc, probe, d_ref, dt_ref, counts, probe_acc, work):
    wave, far, grad, patch = work
    size = probe.shape[-1]
    modes = probe.shape[0] // 2
    blocks = size // LANES
    chunk = 64
    first = jnp.minimum(col // LANES, obj.shape[1] - blocks - 1)
    shift = col - first * LANES
    lane = lax.broadcasted_iota(jnp.int32, (chunk, LANES), 1)
    back_by = lax.rem(LANES - shift, LANES)
    for lo in range(0, size, chunk):
        rows = pl.ds(lo, chunk)
        parts = []
        for plane in range(2):
            rolled = [
                pltpu.roll(obj[plane, first + j, pl.ds(row + lo, chunk), :], back_by, 1)
                for j in range(blocks + 1)
            ]
            part = jnp.concatenate(
                [
                    jnp.where(lane < LANES - shift, rolled[j], rolled[j + 1])
                    for j in range(blocks)
                ],
                axis=1,
            )
            patch[plane, rows, :] = part
            parts.append(part)
        o_re, o_im = parts
        for m in range(modes):
            p_re = probe[2 * m, rows, :]
            p_im = probe[2 * m + 1, rows, :]
            wave[pl.ds(m * size + lo, chunk), :size] = (p_re * o_re - p_im * o_im).astype(
                jnp.bfloat16
            )
            wave[pl.ds(m * size + lo, chunk), size:] = (p_re * o_im + p_im * o_re).astype(
                jnp.bfloat16
            )
    for part in range(2):
        half = jnp.dot(
            wave[...], d_ref[:, part * size : (part + 1) * size], preferred_element_type=jnp.float32
        ).astype(jnp.bfloat16)
        for m in range(modes):
            grad[part * size : (part + 1) * size, m * size : (m + 1) * size] = half[
                m * size : (m + 1) * size
            ]
    for m in range(modes):
        far[:, m * size : (m + 1) * size] = jnp.dot(
            dt_ref[...], grad[:, m * size : (m + 1) * size], preferred_element_type=jnp.float32
        )
    step = 16
    for lo in range(0, size, step):
        re = [far[pl.ds(lo, step), m * size : (m + 1) * size] for m in range(modes)]
        im = [far[pl.ds(size + lo, step), m * size : (m + 1) * size] for m in range(modes)]
        power = 1.0
        for m in range(modes):
            power = power + (re[m] * re[m] + im[m] * im[m])
        count = counts[pl.ds(lo, step), :].astype(jnp.float32)
        ratio = count * lax.rsqrt(jnp.maximum(count, 1.0) * power)
        factor = 2.0 * loss_scale - (2.0 * loss_scale) * ratio
        for m in range(modes):
            grad[pl.ds(lo, step), m * size : (m + 1) * size] = (re[m] * factor).astype(jnp.bfloat16)
            grad[pl.ds(size + lo, step), m * size : (m + 1) * size] = (im[m] * factor).astype(
                jnp.bfloat16
            )
    for m in range(modes):
        back = jnp.dot(
            d_ref[...], grad[:, m * size : (m + 1) * size], preferred_element_type=jnp.float32
        ).astype(jnp.bfloat16)
        for part in range(2):
            wave[m * size : (m + 1) * size, part * size : (part + 1) * size] = back[
                part * size : (part + 1) * size
            ]
    for part in range(2):
        far[:, part * size : (part + 1) * size] = jnp.dot(
            wave[...], dt_ref[:, part * size : (part + 1) * size], preferred_element_type=jnp.float32
        )
    step = 32
    lane = lax.broadcasted_iota(jnp.int32, (step, LANES), 1)
    forth_by = lax.rem(shift, LANES)
    for lo in range(0, size, step):
        rows = pl.ds(lo, step)
        sums = None
        o_re = patch[0, rows, :]
        o_im = patch[1, rows, :]
        for m in range(modes):
            g_re = far[pl.ds(m * size + lo, step), :size]
            g_im = far[pl.ds(m * size + lo, step), size:]
            p_re = probe[2 * m, rows, :]
            p_im = probe[2 * m + 1, rows, :]
            probe_acc[2 * m, rows, :] += o_re * g_re + o_im * g_im
            probe_acc[2 * m + 1, rows, :] += o_re * g_im - o_im * g_re
            term = (p_re * g_re + p_im * g_im, p_re * g_im - p_im * g_re)
            sums = term if sums is None else (sums[0] + term[0], sums[1] + term[1])
        for plane in range(2):
            rolled = [
                pltpu.roll(sums[plane][:, j * LANES : (j + 1) * LANES], forth_by, 1)
                for j in range(blocks)
            ]
            for j in range(blocks + 1):
                left = rolled[j - 1] if j > 0 else 0.0
                right = rolled[j] if j < blocks else 0.0
                acc[plane, first + j, pl.ds(row + lo, step), :] += jnp.where(
                    lane >= shift, right, left
                )


def column_copies(source, target, sem, rows_from, rows_to, count):
    out = []
    for j in range(target.shape[1] if len(target.shape) == 4 else source.shape[1]):
        if len(target.shape) == 4:
            a = source.at[:, pl.ds(rows_from, count), pl.ds(j * LANES, LANES)]
            b = target.at[:, j, pl.ds(rows_to, count), :]
        else:
            a = source.at[:, j, pl.ds(rows_from, count), :]
            b = target.at[:, pl.ds(rows_to, count), pl.ds(j * LANES, LANES)]
        out.append(pltpu.make_async_copy(a, b, sem))
    return out


def inner_kernel(
    offs, cnt, obj_hbm, probe, d_ref, dt_ref, meas_hbm, acc, probe_acc,
    obj, counts, wave, far, grad, patch, sem_obj, sem_meas,
):
    size = probe.shape[-1]
    strip = obj.shape[2]
    slots = meas_hbm.shape[1]
    copies = column_copies(obj_hbm, obj, sem_obj, 0, 0, strip)
    for c in copies:
        c.start()
    used = cnt[0]

    def is_mine(s):
        return jnp.logical_and(s < used, offs[0, s, 0] <= strip - size)

    def fetch(s):
        return pltpu.make_async_copy(meas_hbm.at[0, s], counts.at[s], sem_meas.at[s])

    for s in range(slots):
        @pl.when(is_mine(s))
        def _():
            fetch(s).start()

    acc[...] = jnp.zeros_like(acc)
    probe_acc[...] = jnp.zeros_like(probe_acc)
    for c in copies:
        c.wait()

    @pl.loop(0, used)
    def _(s):
        @pl.when(offs[0, s, 0] <= strip - size)
        def _():
            fetch(s).wait()
            one_slot(
                offs[0, s, 0], offs[0, s, 1], obj, acc, probe, d_ref, dt_ref, counts.at[s],
                probe_acc, (wave, far, grad, patch),
            )


def edge_kernel(
    offs, cnt, obj_hbm, halo, probe, d_ref, dt_ref, meas_hbm, acc_in, probe_in,
    grad_hbm, edge, probe_acc,
    obj, acc, counts, wave, far, grad, patch, sem_obj, sem_meas,
):
    size = probe.shape[-1]
    strip = obj_hbm.shape[1]
    own = strip - size
    slots = meas_hbm.shape[1]
    copies = column_copies(obj_hbm, obj, sem_obj, size, 0, own)
    for c in copies:
        c.start()
    used = cnt[0]

    def fetch(s):
        return pltpu.make_async_copy(meas_hbm.at[0, s], counts.at[s], sem_meas.at[s])

    for s in range(slots):
        @pl.when(jnp.logical_and(s < used, offs[0, s, 0] > own))
        def _():
            fetch(s).start()

    probe_acc[...] = probe_in[...]
    for j in range(obj.shape[1]):
        acc[:, j, :own, :] = acc_in[:, j, size:, :]
        acc[:, j, own:, :] = jnp.zeros((2, size, LANES), jnp.float32)
        obj[:, j, own:, :] = halo[:, :, j * LANES : (j + 1) * LANES].astype(jnp.float32)
    for c in copies:
        c.wait()

    @pl.loop(0, used)
    def _(s):
        @pl.when(offs[0, s, 0] > own)
        def _():
            fetch(s).wait()
            one_slot(
                offs[0, s, 0] - size, offs[0, s, 1], obj, acc, probe, d_ref, dt_ref, counts.at[s],
                probe_acc, (wave, far, grad, patch),
            )

    outs = column_copies(acc, grad_hbm, sem_obj, 0, size, own)
    for c in outs:
        c.start()
    for j in range(obj.shape[1]):
        edge[:, :, j * LANES : (j + 1) * LANES] = acc[:, j, own:, :].astype(jnp.bfloat16)
    for c in outs:
        c.wait()


def final_kernel(grad_in, acc, edge, grad_hbm, stage, sem):
    del grad_in
    size = edge.shape[1]
    copies = []
    for j in range(acc.shape[1]):
        stage[:, j, :, :] = acc[:, j, :size, :] + edge[:, :, j * LANES : (j + 1) * LANES].astype(
            jnp.float32
        )
        copies += [
            pltpu.make_async_copy(
                stage.at[:, j],
                grad_hbm.at[:, pl.ds(0, size), pl.ds(j * LANES, LANES)],
                sem,
            )
        ]
        copies[-1].start()
    for c in copies:
        c.wait()


def reduce_to_shares(flat, axis):
    count = lax.axis_size(axis)
    share = flat.shape[0] // count
    place = lax.axis_index(axis)
    value = flat
    bit = 1
    while bit < count:
        mine = jnp.bitwise_and(place // bit, 1)
        value = value.reshape(-1, 2, share, flat.shape[1])
        keep = lax.dynamic_index_in_dim(value, mine, 1, keepdims=False)
        send = lax.dynamic_index_in_dim(value, 1 - mine, 1, keepdims=False)
        got = lax.ppermute(
            send.astype(jnp.bfloat16), axis, [(s, s ^ bit) for s in range(count)]
        )
        value = keep + got.astype(jnp.float32)
        bit *= 2
    return value.reshape(share, flat.shape[1])


def on_device(object_field, probe_modes, scan_offsets, scan_counts, measured):
    size = probe_modes.shape[-1]
    modes = probe_modes.shape[0]
    strip, cols = object_field.shape[1:]
    slots = measured.shape[1]
    blocks = cols // LANES
    table, table_t = dft_tables(size)
    d_mat = jnp.asarray(table)
    dt_mat = jnp.asarray(table_t)
    probe = probe_modes.reshape(2 * modes, size, size)
    halo = shifted(object_field[:, :size, :].astype(jnp.bfloat16), "tr", -1)

    f32 = jnp.float32
    bf16 = jnp.bfloat16
    vmem = pl.BlockSpec(memory_space=pltpu.VMEM)
    smem = pl.BlockSpec(memory_space=pltpu.SMEM)
    hbm = pl.BlockSpec(memory_space=pl.ANY)
    work = [
        pltpu.VMEM((modes * size, 2 * size), bf16),
        pltpu.VMEM((2 * size, modes * size), f32),
        pltpu.VMEM((2 * size, modes * size), bf16),
        pltpu.VMEM((2, size, size), f32),
    ]
    sems = [pltpu.SemaphoreType.DMA, pltpu.SemaphoreType.DMA((slots,))]
    params = pltpu.CompilerParams(vmem_limit_bytes=36 * 1024 * 1024)
    cost = pl.CostEstimate(
        flops=16 * modes * size * size * size * 4 * slots // 2, bytes_accessed=8 << 20, transcendentals=0
    )
    acc, probe_acc = pl.pallas_call(
        inner_kernel,
        out_shape=(
            jax.ShapeDtypeStruct((2, blocks, strip, LANES), f32),
            jax.ShapeDtypeStruct((2 * modes, size, size), f32),
        ),
        in_specs=[smem, smem, hbm, vmem, vmem, vmem, hbm],
        out_specs=(vmem, vmem),
        scratch_shapes=[
            pltpu.VMEM((2, blocks, strip, LANES), f32),
            pltpu.VMEM((slots, size, size), jnp.int32),
        ]
        + work
        + sems,
        compiler_params=params,
        cost_estimate=cost,
        name="inner",
    )(scan_offsets, scan_counts, object_field, probe, d_mat, dt_mat, measured)
    grad, edge, probe_acc = pl.pallas_call(
        edge_kernel,
        out_shape=(
            jax.ShapeDtypeStruct(object_field.shape, f32),
            jax.ShapeDtypeStruct((2, size, cols), bf16),
            jax.ShapeDtypeStruct((2 * modes, size, size), f32),
        ),
        in_specs=[smem, smem, hbm, vmem, vmem, vmem, vmem, hbm, vmem, vmem],
        out_specs=(hbm, vmem, vmem),
        scratch_shapes=[
            pltpu.VMEM((2, blocks, strip, LANES), f32),
            pltpu.VMEM((2, blocks, strip, LANES), f32),
            pltpu.VMEM((slots, size, size), jnp.int32),
        ]
        + work
        + sems,
        compiler_params=params,
        cost_estimate=cost,
        name="edge",
    )(
        scan_offsets, scan_counts, object_field, halo, probe, d_mat, dt_mat, measured, acc, probe_acc
    )
    edge = shifted(edge, "tr", 1)
    probe_grad = reduce_to_shares(probe_acc.reshape(-1, size), "tr")
    object_grad = pl.pallas_call(
        final_kernel,
        out_shape=jax.ShapeDtypeStruct(object_field.shape, f32),
        in_specs=[hbm, vmem, vmem],
        out_specs=hbm,
        scratch_shapes=[pltpu.VMEM((2, blocks, size, LANES), f32), pltpu.SemaphoreType.DMA],
        input_output_aliases={0: 0},
        compiler_params=pltpu.CompilerParams(vmem_limit_bytes=16 * 1024 * 1024),
        name="finish",
    )(grad, acc, edge)
    return (object_grad, probe_grad)


def solution(mesh):
    return jax.shard_map(
        on_device,
        mesh=mesh,
        in_specs=(
            P(None, ("groups", "tr"), None),
            P(),
            P(("groups", "tr"), None, None),
            P(("groups", "tr")),
            P(("groups", "tr"), None, None, None),
        ),
        out_specs=(P(None, ("groups", "tr"), None), P(("groups", "tr"), None)),
        check_vma=False,
    )
```

```python
import functools

import jax
import jax.numpy as jnp
import ml_dtypes
import numpy as np
from jax import lax
from jax.experimental import pallas as pl
from jax.experimental.pallas import tpu as pltpu
from jax.sharding import PartitionSpec as P

loss_scale = 1.0 / 1024.0
LANES = 128


def shifted(value, axis, steps):
    count = lax.axis_size(axis)
    initial, last = (max(0, -steps), min(count, count - steps))
    return lax.ppermute(value, axis, [(source, source + steps) for source in range(initial, last)])


def dft_tables(size):
    index = np.arange(size)
    angle = -2.0 * np.pi / size * (index[:, None] * index[None, :] % size)
    scale = 1.0 / np.sqrt(size)
    real = np.cos(angle) * scale
    imag = np.sin(angle) * scale
    table = np.block([[real, imag], [-imag, real]]).astype(np.float32)
    table = table.astype(ml_dtypes.bfloat16)
    return table, np.ascontiguousarray(table.T)


def one_slot(row, col, obj, acc, probe, d_ref, dt_ref, counts, wait_counts, probe_acc, work):
    wave, far, grad, patch = work
    size = probe.shape[-1]
    modes = probe.shape[0] // 2
    blocks = size // LANES
    chunk = 64
    first = jnp.minimum(col // LANES, obj.shape[1] - blocks - 1)
    shift = col - first * LANES
    lane = lax.broadcasted_iota(jnp.int32, (chunk, LANES), 1)
    back_by = lax.rem(LANES - shift, LANES)
    for lo in range(0, size, chunk):
        rows = pl.ds(lo, chunk)
        parts = []
        for plane in range(2):
            rolled = [
                pltpu.roll(obj[plane, first + j, pl.ds(row + lo, chunk), :], back_by, 1)
                for j in range(blocks + 1)
            ]
            part = jnp.concatenate(
                [
                    jnp.where(lane < LANES - shift, rolled[j], rolled[j + 1])
                    for j in range(blocks)
                ],
                axis=1,
            )
            patch[plane, rows, :] = part
            parts.append(part)
        o_re, o_im = parts
        for m in range(modes):
            p_re = probe[2 * m, rows, :]
            p_im = probe[2 * m + 1, rows, :]
            wave[pl.ds(m * size + lo, chunk), :size] = (p_re * o_re - p_im * o_im).astype(
                jnp.bfloat16
            )
            wave[pl.ds(m * size + lo, chunk), size:] = (p_re * o_im + p_im * o_re).astype(
                jnp.bfloat16
            )
    for part in range(2):
        half = jnp.dot(
            wave[...], d_ref[:, part * size : (part + 1) * size], preferred_element_type=jnp.float32
        ).astype(jnp.bfloat16)
        for m in range(modes):
            grad[part * size : (part + 1) * size, m * size : (m + 1) * size] = half[
                m * size : (m + 1) * size
            ]
    for m in range(modes):
        far[:, m * size : (m + 1) * size] = jnp.dot(
            dt_ref[...], grad[:, m * size : (m + 1) * size], preferred_element_type=jnp.float32
        )
    wait_counts()
    step = 16
    for lo in range(0, size, step):
        re = [far[pl.ds(lo, step), m * size : (m + 1) * size] for m in range(modes)]
        im = [far[pl.ds(size + lo, step), m * size : (m + 1) * size] for m in range(modes)]
        power = 1.0
        for m in range(modes):
            power = power + (re[m] * re[m] + im[m] * im[m])
        count = counts[pl.ds(lo, step), :].astype(jnp.float32)
        ratio = count * lax.rsqrt(jnp.maximum(count, 1.0) * power)
        factor = 2.0 * loss_scale - (2.0 * loss_scale) * ratio
        for m in range(modes):
            grad[pl.ds(lo, step), m * size : (m + 1) * size] = (re[m] * factor).astype(jnp.bfloat16)
            grad[pl.ds(size + lo, step), m * size : (m + 1) * size] = (im[m] * factor).astype(
                jnp.bfloat16
            )
    for m in range(modes):
        back = jnp.dot(
            d_ref[...], grad[:, m * size : (m + 1) * size], preferred_element_type=jnp.float32
        ).astype(jnp.bfloat16)
        for part in range(2):
            wave[m * size : (m + 1) * size, part * size : (part + 1) * size] = back[
                part * size : (part + 1) * size
            ]
    for part in range(2):
        far[:, part * size : (part + 1) * size] = jnp.dot(
            wave[...], dt_ref[:, part * size : (part + 1) * size], preferred_element_type=jnp.float32
        )
    step = 32
    lane = lax.broadcasted_iota(jnp.int32, (step, LANES), 1)
    forth_by = lax.rem(shift, LANES)
    for lo in range(0, size, step):
        rows = pl.ds(lo, step)
        sums = None
        o_re = patch[0, rows, :]
        o_im = patch[1, rows, :]
        for m in range(modes):
            g_re = far[pl.ds(m * size + lo, step), :size]
            g_im = far[pl.ds(m * size + lo, step), size:]
            p_re = probe[2 * m, rows, :]
            p_im = probe[2 * m + 1, rows, :]
            probe_acc[2 * m, rows, :] += o_re * g_re + o_im * g_im
            probe_acc[2 * m + 1, rows, :] += o_re * g_im - o_im * g_re
            term = (p_re * g_re + p_im * g_im, p_re * g_im - p_im * g_re)
            sums = term if sums is None else (sums[0] + term[0], sums[1] + term[1])
        for plane in range(2):
            rolled = [
                pltpu.roll(sums[plane][:, j * LANES : (j + 1) * LANES], forth_by, 1)
                for j in range(blocks)
            ]
            for j in range(blocks + 1):
                left = rolled[j - 1] if j > 0 else 0.0
                right = rolled[j] if j < blocks else 0.0
                acc[plane, first + j, pl.ds(row + lo, step), :] += jnp.where(
                    lane >= shift, right, left
                )


def counts_copy(meas_hbm, counts, sem, s):
    return pltpu.make_async_copy(meas_hbm.at[0, s], counts.at[s], sem.at[s])


def inner_kernel(
    offs, cnt, obj_hbm, probe_hbm, d_hbm, dt_hbm, meas_hbm,
    obj, acc, probe_acc, probe, d_ref, dt_ref,
    counts, wave, far, grad, patch, sem_obj, sem_meas,
):
    size = probe.shape[-1]
    strip = obj_hbm.shape[1]
    slots = meas_hbm.shape[1]
    copies = [
        pltpu.make_async_copy(
            obj_hbm.at[:, :, pl.ds(j * LANES, LANES)], obj.at[:, j, pl.ds(0, strip), :], sem_obj
        )
        for j in range(obj.shape[1])
    ]
    copies += [
        pltpu.make_async_copy(probe_hbm, probe, sem_obj),
        pltpu.make_async_copy(d_hbm, d_ref, sem_obj),
        pltpu.make_async_copy(dt_hbm, dt_ref, sem_obj),
    ]
    for c in copies:
        c.start()
    used = cnt[0]

    for s in range(slots):

        @pl.when(jnp.logical_and(s < used, offs[0, s, 0] <= strip - size))
        def _():
            counts_copy(meas_hbm, counts, sem_meas, s).start()

    acc[...] = jnp.zeros_like(acc)
    probe_acc[...] = jnp.zeros_like(probe_acc)
    for c in copies:
        c.wait()

    @pl.loop(0, used)
    def _(s):
        @pl.when(offs[0, s, 0] <= strip - size)
        def _():
            one_slot(
                offs[0, s, 0], offs[0, s, 1], obj, acc, probe, d_ref, dt_ref, counts.at[s],
                counts_copy(meas_hbm, counts, sem_meas, s).wait,
                probe_acc, (wave, far, grad, patch),
            )


def edge_kernel(
    axis, offs, cnt, halo, obj_in, acc_in, probe_in, probe, d_ref, dt_ref, meas_hbm,
    obj, acc, edge_top, edge_low, keep, send, probe_acc,
    counts, wave, far, grad, patch, sem_meas,
):
    del obj_in, acc_in, probe_in
    size = probe.shape[-1]
    strip = obj.shape[2] - size
    slots = meas_hbm.shape[1]
    used = cnt[0]

    for s in range(slots):

        @pl.when(jnp.logical_and(s < used, offs[0, s, 0] > strip - size))
        def _():
            counts_copy(meas_hbm, counts, sem_meas, s).start()

    for j in range(obj.shape[1]):
        obj[:, j, strip:, :] = halo[:, :, j * LANES : (j + 1) * LANES].astype(jnp.float32)

    @pl.loop(0, used)
    def _(s):
        @pl.when(offs[0, s, 0] > strip - size)
        def _():
            one_slot(
                offs[0, s, 0], offs[0, s, 1], obj, acc, probe, d_ref, dt_ref, counts.at[s],
                counts_copy(meas_hbm, counts, sem_meas, s).wait,
                probe_acc, (wave, far, grad, patch),
            )

    half = size // 2
    for j in range(obj.shape[1]):
        cols = slice(j * LANES, (j + 1) * LANES)
        edge_top[:, :, cols] = acc[:, j, strip : strip + half, :].astype(jnp.bfloat16)
        edge_low[:, :, cols] = acc[:, j, strip + half :, :].astype(jnp.bfloat16)
    mine = lax.rem(lax.axis_index(axis), 2)
    blocks, share = keep.shape[:2]
    flat = probe_acc.reshape(2 * blocks * share, size)
    for k in range(blocks):
        keep[k] = flat[pl.ds(pl.multiple_of((2 * k + mine) * share, share), share), :]
        send[k] = flat[pl.ds(pl.multiple_of((2 * k + 1 - mine) * share, share), share), :].astype(
            jnp.bfloat16
        )


def split_kernel(axis, bit, value, got, keep, send):
    mine = lax.rem(lax.axis_index(axis) // bit, 2)
    keep[...] = value[:, mine] + got[:, mine].astype(jnp.float32)
    send[...] = (value[:, 1 - mine] + got[:, 1 - mine].astype(jnp.float32)).astype(jnp.bfloat16)


def lower_kernel(acc, grad_hbm, sem):
    strip = grad_hbm.shape[1]
    start = acc.shape[2] - strip
    copies = [
        pltpu.make_async_copy(
            acc.at[:, j, pl.ds(start, strip - start), :],
            grad_hbm.at[:, pl.ds(start, strip - start), pl.ds(j * LANES, LANES)],
            sem,
        )
        for j in range(acc.shape[1])
    ]
    for c in copies:
        c.start()
    for c in copies:
        c.wait()


def final_kernel(grad_in, acc, edge_top, edge_low, mine, other, grad_hbm, probe_grad, stage, sem):
    del grad_in
    half = edge_top.shape[1]
    copies = []
    for j in range(acc.shape[1]):
        cols = slice(j * LANES, (j + 1) * LANES)
        stage[:, j, :half, :] = acc[:, j, :half, :] + edge_top[:, :, cols].astype(jnp.float32)
        stage[:, j, half:, :] = acc[:, j, half : 2 * half, :] + edge_low[:, :, cols].astype(
            jnp.float32
        )
        copies += [
            pltpu.make_async_copy(
                stage.at[:, j],
                grad_hbm.at[:, pl.ds(0, 2 * half), pl.ds(j * LANES, LANES)],
                sem,
            )
        ]
        copies[-1].start()
    probe_grad[...] = mine[...] + other[...].astype(jnp.float32)
    for c in copies:
        c.wait()


def reduce_and_pass_edges(keep, send, edges, axis, params):
    vmem = pl.BlockSpec(memory_space=pltpu.VMEM)
    devices = lax.axis_size(axis)
    blocks, share, lanes = keep.shape
    arrived = []
    bit = 1
    while True:
        stage = bit.bit_length() - 1
        if stage in (1, 2):
            edge = edges[stage - 1]
            edge, send = lax.optimization_barrier((edge, send))
            arrived.append(shifted(edge, axis, 1))
        got = lax.ppermute(send, axis, [(s, s ^ bit) for s in range(devices)])
        bit *= 2
        if bit >= devices:
            return keep, got, arrived
        blocks //= 2
        shape = (blocks, 2, share, lanes)
        keep, send = pl.pallas_call(
            functools.partial(split_kernel, axis, bit),
            out_shape=(
                jax.ShapeDtypeStruct((blocks, share, lanes), jnp.float32),
                jax.ShapeDtypeStruct((blocks, share, lanes), jnp.bfloat16),
            ),
            in_specs=[vmem, vmem],
            out_specs=(vmem, vmem),
            compiler_params=params,
            name="split",
        )(keep.reshape(shape), got.reshape(shape))


def gradients(object_field, probe_modes, scan_offsets, scan_counts, measured):
    size = probe_modes.shape[-1]
    modes = probe_modes.shape[0]
    strip, cols = object_field.shape[1:]
    slots = measured.shape[1]
    blocks = cols // LANES
    table, table_t = dft_tables(size)
    d_mat = jnp.asarray(table)
    dt_mat = jnp.asarray(table_t)
    probe = probe_modes.reshape(2 * modes, size, size)
    halo = shifted(object_field[:, :size, :].astype(jnp.bfloat16), "tr", -1)

    f32 = jnp.float32
    bf16 = jnp.bfloat16
    vmem = pl.BlockSpec(memory_space=pltpu.VMEM)
    smem = pl.BlockSpec(memory_space=pltpu.SMEM)
    hbm = pl.BlockSpec(memory_space=pltpu.HBM)
    work = [
        pltpu.VMEM((slots, size, size), jnp.int32),
        pltpu.VMEM((modes * size, 2 * size), bf16),
        pltpu.VMEM((2 * size, modes * size), f32),
        pltpu.VMEM((2 * size, modes * size), bf16),
        pltpu.VMEM((2, size, size), f32),
    ]
    params = pltpu.CompilerParams(vmem_limit_bytes=16 * 1024 * 1024)
    cost = pl.CostEstimate(
        flops=16 * modes * size * size * size * 4 * slots // 2, bytes_accessed=8 << 20, transcendentals=0
    )
    in_hbm = lambda x: pltpu.with_memory_space_constraint(x, pltpu.HBM)
    probe, d_mat, dt_mat = in_hbm(probe), in_hbm(d_mat), in_hbm(dt_mat)
    object_hbm, measured = in_hbm(object_field), in_hbm(measured)
    tall = jax.ShapeDtypeStruct((2, blocks, strip + size, LANES), f32)
    planes = jax.ShapeDtypeStruct((2 * modes, size, size), f32)
    square = jax.ShapeDtypeStruct((2 * size, 2 * size), bf16)
    obj, acc, probe_acc, probe, d_mat, dt_mat = pl.pallas_call(
        inner_kernel,
        out_shape=(tall, tall, planes, planes, square, square),
        in_specs=[smem, smem, hbm, hbm, hbm, hbm, hbm],
        out_specs=(vmem,) * 6,
        scratch_shapes=work + [pltpu.SemaphoreType.DMA, pltpu.SemaphoreType.DMA((slots,))],
        compiler_params=params,
        cost_estimate=cost,
        name="inner",
    )(scan_offsets, scan_counts, object_hbm, probe, d_mat, dt_mat, measured)
    devices = lax.axis_size("tr")
    shares = (devices // 2, 2 * modes * size // devices, size)
    _, acc, edge_top, edge_low, keep, send, _ = pl.pallas_call(
        functools.partial(edge_kernel, "tr"),
        out_shape=(
            tall,
            tall,
            jax.ShapeDtypeStruct((2, size // 2, cols), bf16),
            jax.ShapeDtypeStruct((2, size // 2, cols), bf16),
            jax.ShapeDtypeStruct(shares, f32),
            jax.ShapeDtypeStruct(shares, bf16),
            planes,
        ),
        in_specs=[smem, smem, vmem, vmem, vmem, vmem, vmem, vmem, vmem, hbm],
        out_specs=(vmem,) * 7,
        scratch_shapes=work + [pltpu.SemaphoreType.DMA((slots,))],
        input_output_aliases={3: 0, 4: 1, 5: 6},
        compiler_params=params,
        cost_estimate=cost,
        name="edge",
    )(scan_offsets, scan_counts, halo, obj, acc, probe_acc, probe, d_mat, dt_mat, measured)
    small = pltpu.CompilerParams(vmem_limit_bytes=8 * 1024 * 1024)
    own, other, edges = reduce_and_pass_edges(keep, send, (edge_top, edge_low), "tr", small)
    grad = pl.pallas_call(
        lower_kernel,
        out_shape=jax.ShapeDtypeStruct(object_field.shape, f32),
        in_specs=[vmem],
        out_specs=hbm,
        scratch_shapes=[pltpu.SemaphoreType.DMA],
        compiler_params=small,
        name="lower",
    )(acc)
    return pl.pallas_call(
        final_kernel,
        out_shape=(
            jax.ShapeDtypeStruct(object_field.shape, f32),
            jax.ShapeDtypeStruct(own.shape[1:], f32),
        ),
        in_specs=[hbm, vmem, vmem, vmem, vmem, vmem],
        out_specs=(hbm, vmem),
        scratch_shapes=[pltpu.VMEM((2, blocks, size, LANES), f32), pltpu.SemaphoreType.DMA],
        input_output_aliases={0: 0},
        compiler_params=small,
        name="finish",
    )(grad, acc, *edges, own[0], other[0])


def solution(mesh):
    return jax.shard_map(
        gradients,
        mesh=mesh,
        in_specs=(
            P(None, ("groups", "tr"), None),
            P(),
            P(("groups", "tr"), None, None),
            P(("groups", "tr")),
            P(("groups", "tr"), None, None, None),
        ),
        out_specs=(P(None, ("groups", "tr"), None), P(("groups", "tr"), None)),
        check_vma=False,
    )
```

```python
import functools

import jax
import jax.numpy as jnp
import ml_dtypes
import numpy as np
from jax import lax
from jax.experimental import pallas as pl
from jax.experimental.pallas import tpu as pltpu
from jax.sharding import PartitionSpec as P

loss_scale = 1.0 / 1024.0
LANES = 128


def shifted(value, axis, steps):
    count = lax.axis_size(axis)
    initial, last = (max(0, -steps), min(count, count - steps))
    return lax.ppermute(value, axis, [(source, source + steps) for source in range(initial, last)])


def dft_tables(size):
    index = np.arange(size)
    angle = -2.0 * np.pi / size * (index[:, None] * index[None, :] % size)
    scale = 1.0 / np.sqrt(size)
    real = np.cos(angle) * scale
    imag = np.sin(angle) * scale
    table = np.block([[real, imag], [-imag, real]]).astype(np.float32)
    table = table.astype(ml_dtypes.bfloat16)
    return table, np.ascontiguousarray(table.T)


def one_slot(row, col, obj, acc, probe, d_ref, dt_ref, counts, wait_counts, probe_acc, work):
    wave, far, grad, patch, probe_low = work
    size = probe.shape[-1]
    modes = probe.shape[0] // 2
    blocks = size // LANES
    chunk = 64
    first = jnp.minimum(col // LANES, obj.shape[1] - blocks - 1)
    shift = col - first * LANES
    lane = lax.broadcasted_iota(jnp.int32, (chunk, LANES), 1)
    back_by = lax.rem(LANES - shift, LANES)
    for lo in range(0, size, chunk):
        rows = pl.ds(lo, chunk)
        parts = []
        for plane in range(2):
            rolled = [
                pltpu.roll(obj[plane, first + j, pl.ds(row + lo, chunk), :], back_by, 1)
                for j in range(blocks + 1)
            ]
            part = jnp.concatenate(
                [
                    jnp.where(lane < LANES - shift, rolled[j], rolled[j + 1])
                    for j in range(blocks)
                ],
                axis=1,
            )
            patch[plane, rows, :] = part.astype(jnp.bfloat16)
            parts.append(part)
        o_re, o_im = parts
        for m in range(modes):
            p_re = probe[2 * m, rows, :]
            p_im = probe[2 * m + 1, rows, :]
            wave[pl.ds(m * size + lo, chunk), :size] = (p_re * o_re - p_im * o_im).astype(
                jnp.bfloat16
            )
            wave[pl.ds(m * size + lo, chunk), size:] = (p_re * o_im + p_im * o_re).astype(
                jnp.bfloat16
            )
    for part in range(2):
        half = jnp.dot(
            wave[...], d_ref[:, part * size : (part + 1) * size], preferred_element_type=jnp.float32
        ).astype(jnp.bfloat16)
        for m in range(modes):
            grad[part * size : (part + 1) * size, m * size : (m + 1) * size] = half[
                m * size : (m + 1) * size
            ]
    for m in range(modes):
        far[:, m * size : (m + 1) * size] = jnp.dot(
            dt_ref[...], grad[:, m * size : (m + 1) * size], preferred_element_type=jnp.float32
        )
    wait_counts()
    step = 16
    for lo in range(0, size, step):
        re = [far[pl.ds(lo, step), m * size : (m + 1) * size] for m in range(modes)]
        im = [far[pl.ds(size + lo, step), m * size : (m + 1) * size] for m in range(modes)]
        power = 1.0
        for m in range(modes):
            power = power + (re[m] * re[m] + im[m] * im[m])
        count = counts[pl.ds(lo, step), :].astype(jnp.float32)
        ratio = count * lax.rsqrt(jnp.maximum(count, 1.0) * power)
        factor = 2.0 * loss_scale - (2.0 * loss_scale) * ratio
        for m in range(modes):
            grad[pl.ds(lo, step), m * size : (m + 1) * size] = (re[m] * factor).astype(jnp.bfloat16)
            grad[pl.ds(size + lo, step), m * size : (m + 1) * size] = (im[m] * factor).astype(
                jnp.bfloat16
            )
    for m in range(modes):
        back = jnp.dot(
            d_ref[...], grad[:, m * size : (m + 1) * size], preferred_element_type=jnp.float32
        ).astype(jnp.bfloat16)
        for part in range(2):
            wave[m * size : (m + 1) * size, part * size : (part + 1) * size] = back[
                part * size : (part + 1) * size
            ]
    for part in range(2):
        grad[:, part * size : (part + 1) * size] = jnp.dot(
            wave[...], dt_ref[:, part * size : (part + 1) * size], preferred_element_type=jnp.float32
        ).astype(jnp.bfloat16)
    step = 32
    lane = lax.broadcasted_iota(jnp.int32, (step, LANES), 1)
    forth_by = lax.rem(shift, LANES)
    for lo in range(0, size, step):
        rows = pl.ds(lo, step)
        sums = None
        o_re = patch[0, rows, :]
        o_im = patch[1, rows, :]
        for m in range(modes):
            g_re = grad[pl.ds(m * size + lo, step), :size]
            g_im = grad[pl.ds(m * size + lo, step), size:]
            p_re = probe_low[2 * m, rows, :]
            p_im = probe_low[2 * m + 1, rows, :]
            probe_acc[2 * m, rows, :] += (o_re * g_re + o_im * g_im).astype(jnp.float32)
            probe_acc[2 * m + 1, rows, :] += (o_re * g_im - o_im * g_re).astype(jnp.float32)
            term = (p_re * g_re + p_im * g_im, p_re * g_im - p_im * g_re)
            sums = term if sums is None else (sums[0] + term[0], sums[1] + term[1])
        for plane in range(2):
            rolled = [
                pltpu.roll(
                sums[plane][:, j * LANES : (j + 1) * LANES].astype(jnp.float32), forth_by, 1
            )
                for j in range(blocks)
            ]
            for j in range(blocks + 1):
                left = rolled[j - 1] if j > 0 else 0.0
                right = rolled[j] if j < blocks else 0.0
                acc[plane, first + j, pl.ds(row + lo, step), :] += jnp.where(
                    lane >= shift, right, left
                )


def counts_copy(meas_hbm, counts, sem, s):
    return pltpu.make_async_copy(meas_hbm.at[0, s], counts.at[s], sem.at[s])


def inner_kernel(
    offs, cnt, obj_hbm, probe_hbm, d_hbm, dt_hbm, meas_hbm,
    obj, acc, probe_acc, probe, d_ref, dt_ref,
    counts, wave, far, grad, patch, probe_low, sem_obj, sem_meas,
):
    size = probe.shape[-1]
    strip = obj_hbm.shape[1]
    slots = meas_hbm.shape[1]
    copies = [
        pltpu.make_async_copy(
            obj_hbm.at[:, :, pl.ds(j * LANES, LANES)], obj.at[:, j, pl.ds(0, strip), :], sem_obj
        )
        for j in range(obj.shape[1])
    ]
    copies += [
        pltpu.make_async_copy(probe_hbm, probe, sem_obj),
        pltpu.make_async_copy(d_hbm, d_ref, sem_obj),
        pltpu.make_async_copy(dt_hbm, dt_ref, sem_obj),
    ]
    for c in copies:
        c.start()
    used = cnt[0]

    for s in range(slots):

        @pl.when(jnp.logical_and(s < used, offs[0, 0, s] <= strip - size))
        def _():
            counts_copy(meas_hbm, counts, sem_meas, s).start()

    acc[...] = jnp.zeros_like(acc)
    probe_acc[...] = jnp.zeros_like(probe_acc)
    for c in copies:
        c.wait()
    probe_low[...] = probe[...].astype(jnp.bfloat16)

    @pl.loop(0, used)
    def _(s):
        @pl.when(offs[0, 0, s] <= strip - size)
        def _():
            one_slot(
                offs[0, 0, s], offs[0, 1, s], obj, acc, probe, d_ref, dt_ref, counts.at[s],
                counts_copy(meas_hbm, counts, sem_meas, s).wait,
                probe_acc, (wave, far, grad, patch, probe_low),
            )


def edge_kernel(
    axis, offs, cnt, halo, obj_in, acc_in, probe_in, probe, d_ref, dt_ref, meas_hbm,
    obj, acc, edge_top, edge_low, keep, send, probe_acc,
    counts, wave, far, grad, patch, probe_low, sem_meas,
):
    del obj_in, acc_in, probe_in
    size = probe.shape[-1]
    strip = obj.shape[2] - size
    slots = meas_hbm.shape[1]
    used = cnt[0]

    for s in range(slots):

        @pl.when(jnp.logical_and(s < used, offs[0, 0, s] > strip - size))
        def _():
            counts_copy(meas_hbm, counts, sem_meas, s).start()

    probe_low[...] = probe[...].astype(jnp.bfloat16)
    for j in range(obj.shape[1]):
        obj[:, j, strip:, :] = halo[:, :, j * LANES : (j + 1) * LANES].astype(jnp.float32)

    @pl.loop(0, used)
    def _(s):
        @pl.when(offs[0, 0, s] > strip - size)
        def _():
            one_slot(
                offs[0, 0, s], offs[0, 1, s], obj, acc, probe, d_ref, dt_ref, counts.at[s],
                counts_copy(meas_hbm, counts, sem_meas, s).wait,
                probe_acc, (wave, far, grad, patch, probe_low),
            )

    half = size // 2
    for j in range(obj.shape[1]):
        cols = slice(j * LANES, (j + 1) * LANES)
        edge_top[:, :, cols] = acc[:, j, strip : strip + half, :].astype(jnp.bfloat16)
        edge_low[:, :, cols] = acc[:, j, strip + half :, :].astype(jnp.bfloat16)
    mine = lax.rem(lax.axis_index(axis), 2)
    blocks, share = keep.shape[:2]
    flat = probe_acc.reshape(2 * blocks * share, size)
    for k in range(blocks):
        keep[k] = flat[pl.ds(pl.multiple_of((2 * k + mine) * share, share), share), :]
        send[k] = flat[pl.ds(pl.multiple_of((2 * k + 1 - mine) * share, share), share), :].astype(
            jnp.bfloat16
        )


def split_kernel(axis, bit, value, got, keep, send):
    mine = lax.rem(lax.axis_index(axis) // bit, 2)
    keep[...] = value[:, mine] + got[:, mine].astype(jnp.float32)
    send[...] = (value[:, 1 - mine] + got[:, 1 - mine].astype(jnp.float32)).astype(jnp.bfloat16)


def lower_kernel(acc, grad_hbm, sem):
    strip = grad_hbm.shape[1]
    start = acc.shape[2] - strip
    copies = [
        pltpu.make_async_copy(
            acc.at[:, j, pl.ds(start, strip - start), :],
            grad_hbm.at[:, pl.ds(start, strip - start), pl.ds(j * LANES, LANES)],
            sem,
        )
        for j in range(acc.shape[1])
    ]
    for c in copies:
        c.start()
    for c in copies:
        c.wait()


def add_edge(at, acc, edge, grad_hbm, stage, sem):
    rows = edge.shape[1]
    copies = []
    for j in range(acc.shape[1]):
        stage[:, j, :, :] = acc[:, j, at : at + rows, :] + edge[
            :, :, j * LANES : (j + 1) * LANES
        ].astype(jnp.float32)
        copies += [
            pltpu.make_async_copy(
                stage.at[:, j], grad_hbm.at[:, pl.ds(at, rows), pl.ds(j * LANES, LANES)], sem
            )
        ]
        copies[-1].start()
    return copies


def top_kernel(grad_in, acc, edge, grad_hbm, stage, sem):
    del grad_in
    for c in add_edge(0, acc, edge, grad_hbm, stage, sem):
        c.wait()


def final_kernel(grad_in, acc, edge, mine, other, grad_hbm, probe_grad, stage, sem):
    del grad_in
    copies = add_edge(edge.shape[1], acc, edge, grad_hbm, stage, sem)
    probe_grad[...] = mine[...] + other[...].astype(jnp.float32)
    for c in copies:
        c.wait()


def reduce_and_pass_edges(keep, send, edges, axis, params):
    vmem = pl.BlockSpec(memory_space=pltpu.VMEM)
    devices = lax.axis_size(axis)
    blocks, share, lanes = keep.shape
    arrived = []
    bit = 1
    while True:
        stage = bit.bit_length() - 1
        if stage in (1, 2):
            edge = edges[stage - 1]
            edge, send = lax.optimization_barrier((edge, send))
            arrived.append(shifted(edge, axis, 1))
        got = lax.ppermute(send, axis, [(s, s ^ bit) for s in range(devices)])
        bit *= 2
        if bit >= devices:
            return keep, got, arrived
        blocks //= 2
        shape = (blocks, 2, share, lanes)
        keep, send = pl.pallas_call(
            functools.partial(split_kernel, axis, bit),
            out_shape=(
                jax.ShapeDtypeStruct((blocks, share, lanes), jnp.float32),
                jax.ShapeDtypeStruct((blocks, share, lanes), jnp.bfloat16),
            ),
            in_specs=[vmem, vmem],
            out_specs=(vmem, vmem),
            compiler_params=params,
            name="split",
        )(keep.reshape(shape), got.reshape(shape))


def gradients(object_field, probe_modes, scan_offsets, scan_counts, measured):
    size = probe_modes.shape[-1]
    modes = probe_modes.shape[0]
    strip, cols = object_field.shape[1:]
    slots = measured.shape[1]
    blocks = cols // LANES
    scan_offsets = jnp.swapaxes(scan_offsets, 1, 2)
    table, table_t = dft_tables(size)
    d_mat = jnp.asarray(table)
    dt_mat = jnp.asarray(table_t)
    probe = probe_modes.reshape(2 * modes, size, size)
    halo = shifted(object_field[:, :size, :].astype(jnp.bfloat16), "tr", -1)

    f32 = jnp.float32
    bf16 = jnp.bfloat16
    vmem = pl.BlockSpec(memory_space=pltpu.VMEM)
    smem = pl.BlockSpec(memory_space=pltpu.SMEM)
    hbm = pl.BlockSpec(memory_space=pltpu.HBM)
    work = [
        pltpu.VMEM((slots, size, size), jnp.int32),
        pltpu.VMEM((modes * size, 2 * size), bf16),
        pltpu.VMEM((2 * size, modes * size), f32),
        pltpu.VMEM((2 * size, modes * size), bf16),
        pltpu.VMEM((2, size, size), bf16),
        pltpu.VMEM((2 * modes, size, size), bf16),
    ]
    params = pltpu.CompilerParams(vmem_limit_bytes=16 * 1024 * 1024)
    cost = pl.CostEstimate(
        flops=16 * modes * size * size * size * 4 * slots // 2, bytes_accessed=8 << 20, transcendentals=0
    )
    in_hbm = lambda x: pltpu.with_memory_space_constraint(x, pltpu.HBM)
    probe, d_mat, dt_mat = in_hbm(probe), in_hbm(d_mat), in_hbm(dt_mat)
    object_hbm, measured = in_hbm(object_field), in_hbm(measured)
    tall = jax.ShapeDtypeStruct((2, blocks, strip + size, LANES), f32)
    planes = jax.ShapeDtypeStruct((2 * modes, size, size), f32)
    square = jax.ShapeDtypeStruct((2 * size, 2 * size), bf16)
    obj, acc, probe_acc, probe, d_mat, dt_mat = pl.pallas_call(
        inner_kernel,
        out_shape=(tall, tall, planes, planes, square, square),
        in_specs=[smem, smem, hbm, hbm, hbm, hbm, hbm],
        out_specs=(vmem,) * 6,
        scratch_shapes=work + [pltpu.SemaphoreType.DMA, pltpu.SemaphoreType.DMA((slots,))],
        compiler_params=params,
        cost_estimate=cost,
        name="inner",
    )(scan_offsets, scan_counts, object_hbm, probe, d_mat, dt_mat, measured)
    devices = lax.axis_size("tr")
    shares = (devices // 2, 2 * modes * size // devices, size)
    _, acc, edge_top, edge_low, keep, send, _ = pl.pallas_call(
        functools.partial(edge_kernel, "tr"),
        out_shape=(
            tall,
            tall,
            jax.ShapeDtypeStruct((2, size // 2, cols), bf16),
            jax.ShapeDtypeStruct((2, size // 2, cols), bf16),
            jax.ShapeDtypeStruct(shares, f32),
            jax.ShapeDtypeStruct(shares, bf16),
            planes,
        ),
        in_specs=[smem, smem, vmem, vmem, vmem, vmem, vmem, vmem, vmem, hbm],
        out_specs=(vmem,) * 7,
        scratch_shapes=work + [pltpu.SemaphoreType.DMA((slots,))],
        input_output_aliases={3: 0, 4: 1, 5: 6},
        compiler_params=params,
        cost_estimate=cost,
        name="edge",
    )(scan_offsets, scan_counts, halo, obj, acc, probe_acc, probe, d_mat, dt_mat, measured)
    small = pltpu.CompilerParams(vmem_limit_bytes=8 * 1024 * 1024)
    own, other, edges = reduce_and_pass_edges(keep, send, (edge_top, edge_low), "tr", small)
    grad = pl.pallas_call(
        lower_kernel,
        out_shape=jax.ShapeDtypeStruct(object_field.shape, f32),
        in_specs=[vmem],
        out_specs=hbm,
        scratch_shapes=[pltpu.SemaphoreType.DMA],
        compiler_params=small,
        name="lower",
    )(acc)
    scratch = [pltpu.VMEM((2, blocks, size // 2, LANES), f32), pltpu.SemaphoreType.DMA]
    grad = pl.pallas_call(
        top_kernel,
        out_shape=jax.ShapeDtypeStruct(object_field.shape, f32),
        in_specs=[hbm, vmem, vmem],
        out_specs=hbm,
        scratch_shapes=scratch,
        input_output_aliases={0: 0},
        compiler_params=small,
        name="top",
    )(grad, acc, edges[0])
    return pl.pallas_call(
        final_kernel,
        out_shape=(
            jax.ShapeDtypeStruct(object_field.shape, f32),
            jax.ShapeDtypeStruct(own.shape[1:], f32),
        ),
        in_specs=[hbm, vmem, vmem, vmem, vmem],
        out_specs=(hbm, vmem),
        scratch_shapes=scratch,
        input_output_aliases={0: 0},
        compiler_params=small,
        name="finish",
    )(grad, acc, edges[1], own[0], other[0])


def solution(mesh):
    return jax.shard_map(
        gradients,
        mesh=mesh,
        in_specs=(
            P(None, ("groups", "tr"), None),
            P(),
            P(("groups", "tr"), None, None),
            P(("groups", "tr")),
            P(("groups", "tr"), None, None, None),
        ),
        out_specs=(P(None, ("groups", "tr"), None), P(("groups", "tr"), None)),
        check_vma=False,
    )
```

```python
import functools

import jax
import jax.numpy as jnp
import ml_dtypes
import numpy as np
from jax import lax
from jax.experimental import pallas as pl
from jax.experimental.pallas import tpu as pltpu
from jax.sharding import PartitionSpec as P

loss_scale = 1.0 / 1024.0
LANES = 128


def shifted(value, axis, steps):
    count = lax.axis_size(axis)
    initial, last = (max(0, -steps), min(count, count - steps))
    return lax.ppermute(value, axis, [(source, source + steps) for source in range(initial, last)])


def dft_tables(size):
    index = np.arange(size)
    angle = -2.0 * np.pi / size * (index[:, None] * index[None, :] % size)
    scale = 1.0 / np.sqrt(size)
    real = np.cos(angle) * scale
    imag = np.sin(angle) * scale
    table = np.block([[real, imag], [-imag, real]]).astype(np.float32)
    table = table.astype(ml_dtypes.bfloat16)
    return table, np.ascontiguousarray(table.T)


def one_slot(row, col, obj, acc, probe, d_ref, dt_ref, counts, wait_counts, probe_acc, work):
    wave, far, grad, patch, probe_low = work
    size = probe.shape[-1]
    modes = probe.shape[0] // 2
    blocks = size // LANES
    chunk = 64
    first = jnp.minimum(col // LANES, obj.shape[1] - blocks - 1)
    shift = col - first * LANES
    lane = lax.broadcasted_iota(jnp.int32, (chunk, LANES), 1)
    back_by = lax.rem(LANES - shift, LANES)
    for lo in range(0, size, chunk):
        rows = pl.ds(lo, chunk)
        parts = []
        for plane in range(2):
            rolled = [
                pltpu.roll(obj[plane, first + j, pl.ds(row + lo, chunk), :], back_by, 1)
                for j in range(blocks + 1)
            ]
            part = jnp.concatenate(
                [
                    jnp.where(lane < LANES - shift, rolled[j], rolled[j + 1])
                    for j in range(blocks)
                ],
                axis=1,
            )
            patch[plane, rows, :] = part.astype(jnp.bfloat16)
            parts.append(part)
        o_re, o_im = parts
        for m in range(modes):
            p_re = probe[2 * m, rows, :]
            p_im = probe[2 * m + 1, rows, :]
            wave[pl.ds(m * size + lo, chunk), :size] = (p_re * o_re - p_im * o_im).astype(
                jnp.bfloat16
            )
            wave[pl.ds(m * size + lo, chunk), size:] = (p_re * o_im + p_im * o_re).astype(
                jnp.bfloat16
            )
    for part in range(2):
        half = jnp.dot(
            wave[...], d_ref[:, part * size : (part + 1) * size], preferred_element_type=jnp.float32
        ).astype(jnp.bfloat16)
        for m in range(modes):
            grad[part * size : (part + 1) * size, m * size : (m + 1) * size] = half[
                m * size : (m + 1) * size
            ]
    for m in range(modes):
        far[:, m * size : (m + 1) * size] = jnp.dot(
            dt_ref[...], grad[:, m * size : (m + 1) * size], preferred_element_type=jnp.float32
        )
    wait_counts()
    step = 16
    for lo in range(0, size, step):
        re = [far[pl.ds(lo, step), m * size : (m + 1) * size] for m in range(modes)]
        im = [far[pl.ds(size + lo, step), m * size : (m + 1) * size] for m in range(modes)]
        power = 1.0
        for m in range(modes):
            power = power + (re[m] * re[m] + im[m] * im[m])
        count = counts[pl.ds(lo, step), :].astype(jnp.float32)
        ratio = count * lax.rsqrt(jnp.maximum(count, 1.0) * power)
        factor = 2.0 * loss_scale - (2.0 * loss_scale) * ratio
        for m in range(modes):
            grad[pl.ds(lo, step), m * size : (m + 1) * size] = (re[m] * factor).astype(jnp.bfloat16)
            grad[pl.ds(size + lo, step), m * size : (m + 1) * size] = (im[m] * factor).astype(
                jnp.bfloat16
            )
    for m in range(modes):
        back = jnp.dot(
            d_ref[...], grad[:, m * size : (m + 1) * size], preferred_element_type=jnp.float32
        ).astype(jnp.bfloat16)
        for part in range(2):
            wave[m * size : (m + 1) * size, part * size : (part + 1) * size] = back[
                part * size : (part + 1) * size
            ]
    for part in range(2):
        grad[:, part * size : (part + 1) * size] = jnp.dot(
            wave[...], dt_ref[:, part * size : (part + 1) * size], preferred_element_type=jnp.float32
        ).astype(jnp.bfloat16)
    step = 32
    lane = lax.broadcasted_iota(jnp.int32, (step, LANES), 1)
    forth_by = lax.rem(shift, LANES)
    for lo in range(0, size, step):
        rows = pl.ds(lo, step)
        sums = None
        o_re = patch[0, rows, :]
        o_im = patch[1, rows, :]
        for m in range(modes):
            g_re = grad[pl.ds(m * size + lo, step), :size]
            g_im = grad[pl.ds(m * size + lo, step), size:]
            p_re = probe_low[2 * m, rows, :]
            p_im = probe_low[2 * m + 1, rows, :]
            probe_acc[2 * m, rows, :] += (o_re * g_re + o_im * g_im).astype(jnp.float32)
            probe_acc[2 * m + 1, rows, :] += (o_re * g_im - o_im * g_re).astype(jnp.float32)
            term = (p_re * g_re + p_im * g_im, p_re * g_im - p_im * g_re)
            sums = term if sums is None else (sums[0] + term[0], sums[1] + term[1])
        for plane in range(2):
            rolled = [
                pltpu.roll(
                sums[plane][:, j * LANES : (j + 1) * LANES].astype(jnp.float32), forth_by, 1
            )
                for j in range(blocks)
            ]
            for j in range(blocks + 1):
                left = rolled[j - 1] if j > 0 else 0.0
                right = rolled[j] if j < blocks else 0.0
                acc[plane, first + j, pl.ds(row + lo, step), :] += jnp.where(
                    lane >= shift, right, left
                )


def counts_copy(meas_hbm, counts, sem, s):
    return pltpu.make_async_copy(meas_hbm.at[0, s], counts.at[s], sem.at[s])


def inner_kernel(
    offs, cnt, obj_hbm, probe_hbm, d_hbm, dt_hbm, meas_hbm,
    obj, acc, probe_acc, probe, d_ref, dt_ref, probe_low,
    counts, wave, far, grad, patch, sem_obj, sem_meas,
):
    size = probe.shape[-1]
    strip = obj_hbm.shape[1]
    slots = meas_hbm.shape[1]
    copies = [
        pltpu.make_async_copy(
            obj_hbm.at[:, :, pl.ds(j * LANES, LANES)], obj.at[:, j, pl.ds(0, strip), :], sem_obj
        )
        for j in range(obj.shape[1])
    ]
    copies += [
        pltpu.make_async_copy(probe_hbm, probe, sem_obj),
        pltpu.make_async_copy(d_hbm, d_ref, sem_obj),
        pltpu.make_async_copy(dt_hbm, dt_ref, sem_obj),
    ]
    for c in copies:
        c.start()
    used = cnt[0]

    for s in range(slots):

        @pl.when(jnp.logical_and(s < used, offs[0, 0, s] <= strip - size))
        def _():
            counts_copy(meas_hbm, counts, sem_meas, s).start()

    acc[...] = jnp.zeros_like(acc)
    probe_acc[...] = jnp.zeros_like(probe_acc)
    for c in copies:
        c.wait()
    probe_low[...] = probe[...].astype(jnp.bfloat16)

    @pl.loop(0, used)
    def _(s):
        @pl.when(offs[0, 0, s] <= strip - size)
        def _():
            one_slot(
                offs[0, 0, s], offs[0, 1, s], obj, acc, probe, d_ref, dt_ref, counts.at[s],
                counts_copy(meas_hbm, counts, sem_meas, s).wait,
                probe_acc, (wave, far, grad, patch, probe_low),
            )


def edge_kernel(
    axis, offs, cnt, halo, obj_in, acc_in, probe_in, probe, probe_low, d_ref, dt_ref, meas_hbm,
    obj, acc, edge_top, edge_low, keep, send, probe_acc,
    counts, wave, far, grad, patch, sem_meas,
):
    del obj_in, acc_in, probe_in
    size = probe.shape[-1]
    strip = obj.shape[2] - size
    slots = meas_hbm.shape[1]
    used = cnt[0]

    for s in range(slots):

        @pl.when(jnp.logical_and(s < used, offs[0, 0, s] > strip - size))
        def _():
            counts_copy(meas_hbm, counts, sem_meas, s).start()

    for j in range(obj.shape[1]):
        obj[:, j, strip:, :] = halo[:, :, j * LANES : (j + 1) * LANES].astype(jnp.float32)

    @pl.loop(0, used)
    def _(s):
        @pl.when(offs[0, 0, s] > strip - size)
        def _():
            one_slot(
                offs[0, 0, s], offs[0, 1, s], obj, acc, probe, d_ref, dt_ref, counts.at[s],
                counts_copy(meas_hbm, counts, sem_meas, s).wait,
                probe_acc, (wave, far, grad, patch, probe_low),
            )

    half = size // 2
    for j in range(obj.shape[1]):
        cols = slice(j * LANES, (j + 1) * LANES)
        edge_top[:, :, cols] = acc[:, j, strip : strip + half, :].astype(jnp.bfloat16)
        edge_low[:, :, cols] = acc[:, j, strip + half :, :].astype(jnp.bfloat16)
    mine = lax.rem(lax.axis_index(axis), 2)
    blocks, share = keep.shape[:2]
    flat = probe_acc.reshape(2 * blocks * share, size)
    for k in range(blocks):
        keep[k] = flat[pl.ds(pl.multiple_of((2 * k + mine) * share, share), share), :]
        send[k] = flat[pl.ds(pl.multiple_of((2 * k + 1 - mine) * share, share), share), :].astype(
            jnp.bfloat16
        )


def split_kernel(axis, bit, value, got, keep, send):
    mine = lax.rem(lax.axis_index(axis) // bit, 2)
    keep[...] = value[:, mine] + got[:, mine].astype(jnp.float32)
    send[...] = (value[:, 1 - mine] + got[:, 1 - mine].astype(jnp.float32)).astype(jnp.bfloat16)


def lower_kernel(acc, grad_hbm, sem):
    strip = grad_hbm.shape[1]
    start = acc.shape[2] - strip
    copies = [
        pltpu.make_async_copy(
            acc.at[:, j, pl.ds(start, strip - start), :],
            grad_hbm.at[:, pl.ds(start, strip - start), pl.ds(j * LANES, LANES)],
            sem,
        )
        for j in range(acc.shape[1])
    ]
    for c in copies:
        c.start()
    for c in copies:
        c.wait()


def add_edge(at, acc, edge, grad_hbm, stage, sem):
    rows = edge.shape[1]
    copies = []
    for j in range(acc.shape[1]):
        stage[:, j, :, :] = acc[:, j, at : at + rows, :] + edge[
            :, :, j * LANES : (j + 1) * LANES
        ].astype(jnp.float32)
        copies += [
            pltpu.make_async_copy(
                stage.at[:, j], grad_hbm.at[:, pl.ds(at, rows), pl.ds(j * LANES, LANES)], sem
            )
        ]
        copies[-1].start()
    return copies


def top_kernel(grad_in, acc, edge, grad_hbm, stage, sem):
    del grad_in
    for c in add_edge(0, acc, edge, grad_hbm, stage, sem):
        c.wait()


def final_kernel(grad_in, acc, edge, mine, other, grad_hbm, probe_hbm, stage, total, sem, sem_probe):
    del grad_in
    total[...] = mine[...] + other[...].astype(jnp.float32)
    whole = pltpu.make_async_copy(total, probe_hbm, sem_probe)
    whole.start()
    for c in add_edge(edge.shape[1], acc, edge, grad_hbm, stage, sem):
        c.wait()
    whole.wait()


def reduce_and_pass_edges(keep, send, edges, axis, params):
    vmem = pl.BlockSpec(memory_space=pltpu.VMEM)
    devices = lax.axis_size(axis)
    blocks, share, lanes = keep.shape
    arrived = []
    bit = 1
    while True:
        stage = bit.bit_length() - 1
        if stage in (1, 2):
            edge = edges[stage - 1]
            edge, send = lax.optimization_barrier((edge, send))
            arrived.append(shifted(edge, axis, 1))
        got = lax.ppermute(send, axis, [(s, s ^ bit) for s in range(devices)])
        bit *= 2
        if bit >= devices:
            return keep, got, arrived
        blocks //= 2
        shape = (blocks, 2, share, lanes)
        keep, send = pl.pallas_call(
            functools.partial(split_kernel, axis, bit),
            out_shape=(
                jax.ShapeDtypeStruct((blocks, share, lanes), jnp.float32),
                jax.ShapeDtypeStruct((blocks, share, lanes), jnp.bfloat16),
            ),
            in_specs=[vmem, vmem],
            out_specs=(vmem, vmem),
            compiler_params=params,
            name="split",
        )(keep.reshape(shape), got.reshape(shape))


def gradients(object_field, probe_modes, scan_offsets, scan_counts, measured):
    size = probe_modes.shape[-1]
    modes = probe_modes.shape[0]
    strip, cols = object_field.shape[1:]
    slots = measured.shape[1]
    blocks = cols // LANES
    scan_offsets = jnp.swapaxes(scan_offsets, 1, 2)
    table, table_t = dft_tables(size)
    d_mat = jnp.asarray(table)
    dt_mat = jnp.asarray(table_t)
    probe = probe_modes.reshape(2 * modes, size, size)
    halo = shifted(object_field[:, :size, :].astype(jnp.bfloat16), "tr", -1)

    f32 = jnp.float32
    bf16 = jnp.bfloat16
    vmem = pl.BlockSpec(memory_space=pltpu.VMEM)
    smem = pl.BlockSpec(memory_space=pltpu.SMEM)
    hbm = pl.BlockSpec(memory_space=pltpu.HBM)
    work = [
        pltpu.VMEM((slots, size, size), jnp.int32),
        pltpu.VMEM((modes * size, 2 * size), bf16),
        pltpu.VMEM((2 * size, modes * size), f32),
        pltpu.VMEM((2 * size, modes * size), bf16),
        pltpu.VMEM((2, size, size), bf16),
    ]
    params = pltpu.CompilerParams(vmem_limit_bytes=16 * 1024 * 1024)
    cost = pl.CostEstimate(
        flops=16 * modes * size * size * size * 4 * slots // 2, bytes_accessed=8 << 20, transcendentals=0
    )
    in_hbm = lambda x: pltpu.with_memory_space_constraint(x, pltpu.HBM)
    probe, d_mat, dt_mat = in_hbm(probe), in_hbm(d_mat), in_hbm(dt_mat)
    object_hbm, measured = in_hbm(object_field), in_hbm(measured)
    tall = jax.ShapeDtypeStruct((2, blocks, strip + size, LANES), f32)
    planes = jax.ShapeDtypeStruct((2 * modes, size, size), f32)
    low_planes = jax.ShapeDtypeStruct(planes.shape, bf16)
    square = jax.ShapeDtypeStruct((2 * size, 2 * size), bf16)
    obj, acc, probe_acc, probe, d_mat, dt_mat, probe_low = pl.pallas_call(
        inner_kernel,
        out_shape=(tall, tall, planes, planes, square, square, low_planes),
        in_specs=[smem, smem, hbm, hbm, hbm, hbm, hbm],
        out_specs=(vmem,) * 7,
        scratch_shapes=work + [pltpu.SemaphoreType.DMA, pltpu.SemaphoreType.DMA((slots,))],
        compiler_params=params,
        cost_estimate=cost,
        name="inner",
    )(scan_offsets, scan_counts, object_hbm, probe, d_mat, dt_mat, measured)
    devices = lax.axis_size("tr")
    shares = (devices // 2, 2 * modes * size // devices, size)
    _, acc, edge_top, edge_low, keep, send, _ = pl.pallas_call(
        functools.partial(edge_kernel, "tr"),
        out_shape=(
            tall,
            tall,
            jax.ShapeDtypeStruct((2, size // 2, cols), bf16),
            jax.ShapeDtypeStruct((2, size // 2, cols), bf16),
            jax.ShapeDtypeStruct(shares, f32),
            jax.ShapeDtypeStruct(shares, bf16),
            planes,
        ),
        in_specs=[smem, smem] + [vmem] * 8 + [hbm],
        out_specs=(vmem,) * 7,
        scratch_shapes=work + [pltpu.SemaphoreType.DMA((slots,))],
        input_output_aliases={3: 0, 4: 1, 5: 6},
        compiler_params=params,
        cost_estimate=cost,
        name="edge",
    )(scan_offsets, scan_counts, halo, obj, acc, probe_acc, probe, probe_low, d_mat, dt_mat, measured)
    small = pltpu.CompilerParams(vmem_limit_bytes=8 * 1024 * 1024)
    own, other, edges = reduce_and_pass_edges(keep, send, (edge_top, edge_low), "tr", small)
    grad = pl.pallas_call(
        lower_kernel,
        out_shape=jax.ShapeDtypeStruct(object_field.shape, f32),
        in_specs=[vmem],
        out_specs=hbm,
        scratch_shapes=[pltpu.SemaphoreType.DMA],
        compiler_params=small,
        name="lower",
    )(acc)
    scratch = [pltpu.VMEM((2, blocks, size // 2, LANES), f32), pltpu.SemaphoreType.DMA]
    grad = pl.pallas_call(
        top_kernel,
        out_shape=jax.ShapeDtypeStruct(object_field.shape, f32),
        in_specs=[hbm, vmem, vmem],
        out_specs=hbm,
        scratch_shapes=scratch,
        input_output_aliases={0: 0},
        compiler_params=small,
        name="top",
    )(grad, acc, edges[0])
    return pl.pallas_call(
        final_kernel,
        out_shape=(
            jax.ShapeDtypeStruct(object_field.shape, f32),
            jax.ShapeDtypeStruct(own.shape[1:], f32),
        ),
        in_specs=[hbm, vmem, vmem, vmem, vmem],
        out_specs=(hbm, hbm),
        scratch_shapes=scratch[:1]
        + [pltpu.VMEM(own.shape[1:], f32), scratch[1], pltpu.SemaphoreType.DMA],
        input_output_aliases={0: 0},
        compiler_params=small,
        name="finish",
    )(grad, acc, edges[1], own[0], other[0])


def solution(mesh):
    return jax.shard_map(
        gradients,
        mesh=mesh,
        in_specs=(
            P(None, ("groups", "tr"), None),
            P(),
            P(("groups", "tr"), None, None),
            P(("groups", "tr")),
            P(("groups", "tr"), None, None, None),
        ),
        out_specs=(P(None, ("groups", "tr"), None), P(("groups", "tr"), None)),
        check_vma=False,
    )
```

```python
import functools

import jax
import jax.numpy as jnp
import ml_dtypes
import numpy as np
from jax import lax
from jax.experimental import pallas as pl
from jax.experimental.pallas import tpu as pltpu
from jax.sharding import PartitionSpec as P

loss_scale = 1.0 / 1024.0
LANES = 128


def shifted(value, axis, steps):
    count = lax.axis_size(axis)
    initial, last = (max(0, -steps), min(count, count - steps))
    return lax.ppermute(value, axis, [(source, source + steps) for source in range(initial, last)])


def dft_tables(size):
    index = np.arange(size)
    angle = -2.0 * np.pi / size * (index[:, None] * index[None, :] % size)
    scale = 1.0 / np.sqrt(size)
    real = np.cos(angle) * scale
    imag = np.sin(angle) * scale
    table = np.block([[real, imag], [-imag, real]]).astype(np.float32)
    table = table.astype(ml_dtypes.bfloat16)
    return table, np.ascontiguousarray(table.T)


def one_slot(row, col, obj, acc, probe, d_ref, dt_ref, counts, wait_counts, probe_acc, work):
    wave, far, grad, patch, probe_low = work
    size = probe.shape[-1]
    modes = probe.shape[0] // 2
    blocks = size // LANES
    chunk = 64
    first = jnp.minimum(col // LANES, obj.shape[1] - blocks - 1)
    shift = col - first * LANES
    lane = lax.broadcasted_iota(jnp.int32, (chunk, LANES), 1)
    back_by = lax.rem(LANES - shift, LANES)
    for lo in range(0, size, chunk):
        rows = pl.ds(lo, chunk)
        parts = []
        for plane in range(2):
            rolled = [
                pltpu.roll(obj[plane, first + j, pl.ds(row + lo, chunk), :], back_by, 1)
                for j in range(blocks + 1)
            ]
            part = jnp.concatenate(
                [
                    jnp.where(lane < LANES - shift, rolled[j], rolled[j + 1])
                    for j in range(blocks)
                ],
                axis=1,
            )
            patch[plane, rows, :] = part.astype(jnp.bfloat16)
            parts.append(part)
        o_re, o_im = parts
        for m in range(modes):
            p_re = probe[2 * m, rows, :]
            p_im = probe[2 * m + 1, rows, :]
            wave[pl.ds(m * size + lo, chunk), :size] = (p_re * o_re - p_im * o_im).astype(
                jnp.bfloat16
            )
            wave[pl.ds(m * size + lo, chunk), size:] = (p_re * o_im + p_im * o_re).astype(
                jnp.bfloat16
            )
    for part in range(2):
        half = jnp.dot(
            wave[...], d_ref[:, part * size : (part + 1) * size], preferred_element_type=jnp.float32
        ).astype(jnp.bfloat16)
        for m in range(modes):
            grad[part * size : (part + 1) * size, m * size : (m + 1) * size] = half[
                m * size : (m + 1) * size
            ]
    for m in range(modes):
        far[:, m * size : (m + 1) * size] = jnp.dot(
            dt_ref[...], grad[:, m * size : (m + 1) * size], preferred_element_type=jnp.float32
        )
    wait_counts()
    step = 16
    for lo in range(0, size, step):
        re = [far[pl.ds(lo, step), m * size : (m + 1) * size] for m in range(modes)]
        im = [far[pl.ds(size + lo, step), m * size : (m + 1) * size] for m in range(modes)]
        power = 1.0
        for m in range(modes):
            power = power + (re[m] * re[m] + im[m] * im[m])
        count = counts[pl.ds(lo, step), :].astype(jnp.float32)
        ratio = count * lax.rsqrt(jnp.maximum(count, 1.0) * power)
        factor = 2.0 * loss_scale - (2.0 * loss_scale) * ratio
        for m in range(modes):
            grad[pl.ds(lo, step), m * size : (m + 1) * size] = (re[m] * factor).astype(jnp.bfloat16)
            grad[pl.ds(size + lo, step), m * size : (m + 1) * size] = (im[m] * factor).astype(
                jnp.bfloat16
            )
    for m in range(modes):
        back = jnp.dot(
            d_ref[...], grad[:, m * size : (m + 1) * size], preferred_element_type=jnp.float32
        ).astype(jnp.bfloat16)
        for part in range(2):
            wave[m * size : (m + 1) * size, part * size : (part + 1) * size] = back[
                part * size : (part + 1) * size
            ]
    for part in range(2):
        grad[:, part * size : (part + 1) * size] = jnp.dot(
            wave[...], dt_ref[:, part * size : (part + 1) * size], preferred_element_type=jnp.float32
        ).astype(jnp.bfloat16)
    step = 32
    lane = lax.broadcasted_iota(jnp.int32, (step, LANES), 1)
    forth_by = lax.rem(shift, LANES)
    for lo in range(0, size, step):
        rows = pl.ds(lo, step)
        sums = None
        o_re = patch[0, rows, :]
        o_im = patch[1, rows, :]
        for m in range(modes):
            g_re = grad[pl.ds(m * size + lo, step), :size]
            g_im = grad[pl.ds(m * size + lo, step), size:]
            p_re = probe_low[2 * m, rows, :]
            p_im = probe_low[2 * m + 1, rows, :]
            probe_acc[2 * m, rows, :] += (o_re * g_re + o_im * g_im).astype(jnp.float32)
            probe_acc[2 * m + 1, rows, :] += (o_re * g_im - o_im * g_re).astype(jnp.float32)
            term = (p_re * g_re + p_im * g_im, p_re * g_im - p_im * g_re)
            sums = term if sums is None else (sums[0] + term[0], sums[1] + term[1])
        for plane in range(2):
            rolled = [
                pltpu.roll(
                sums[plane][:, j * LANES : (j + 1) * LANES].astype(jnp.float32), forth_by, 1
            )
                for j in range(blocks)
            ]
            for j in range(blocks + 1):
                left = rolled[j - 1] if j > 0 else 0.0
                right = rolled[j] if j < blocks else 0.0
                acc[plane, first + j, pl.ds(row + lo, step), :] += jnp.where(
                    lane >= shift, right, left
                )


def counts_copy(meas_hbm, counts, sem, s):
    return pltpu.make_async_copy(meas_hbm.at[0, s], counts.at[s], sem.at[s])


def inner_kernel(
    offs, cnt, obj_hbm, probe_hbm, d_hbm, dt_hbm, meas_hbm,
    obj, acc, probe_acc, probe, d_ref, dt_ref, probe_low,
    counts, wave, far, grad, patch, sem_obj, sem_meas,
):
    size = probe.shape[-1]
    strip = obj_hbm.shape[1]
    slots = meas_hbm.shape[1]
    copies = [
        pltpu.make_async_copy(
            obj_hbm.at[:, :, pl.ds(j * LANES, LANES)], obj.at[:, j, pl.ds(0, strip), :], sem_obj
        )
        for j in range(obj.shape[1])
    ]
    copies += [
        pltpu.make_async_copy(probe_hbm, probe, sem_obj),
        pltpu.make_async_copy(d_hbm, d_ref, sem_obj),
        pltpu.make_async_copy(dt_hbm, dt_ref, sem_obj),
    ]
    for c in copies:
        c.start()
    used = cnt[0]

    for s in range(slots):

        @pl.when(jnp.logical_and(s < used, offs[0, 0, s] <= strip - size))
        def _():
            counts_copy(meas_hbm, counts, sem_meas, s).start()

    acc[...] = jnp.zeros_like(acc)
    probe_acc[...] = jnp.zeros_like(probe_acc)
    for c in copies:
        c.wait()
    probe_low[...] = probe[...].astype(jnp.bfloat16)

    @pl.loop(0, used)
    def _(s):
        @pl.when(offs[0, 0, s] <= strip - size)
        def _():
            one_slot(
                offs[0, 0, s], offs[0, 1, s], obj, acc, probe, d_ref, dt_ref, counts.at[s],
                counts_copy(meas_hbm, counts, sem_meas, s).wait,
                probe_acc, (wave, far, grad, patch, probe_low),
            )


def edge_kernel(
    axis, offs, cnt, halo, obj_in, acc_in, probe_in, probe, probe_low, d_ref, dt_ref, meas_hbm,
    obj, acc, keep, send, probe_acc,
    counts, wave, far, grad, patch, sem_meas,
):
    del obj_in, acc_in, probe_in
    size = probe.shape[-1]
    strip = obj.shape[2] - size
    slots = meas_hbm.shape[1]
    used = cnt[0]

    for s in range(slots):

        @pl.when(jnp.logical_and(s < used, offs[0, 0, s] > strip - size))
        def _():
            counts_copy(meas_hbm, counts, sem_meas, s).start()

    for j in range(obj.shape[1]):
        obj[:, j, strip:, :] = halo[:, :, j * LANES : (j + 1) * LANES].astype(jnp.float32)

    @pl.loop(0, used)
    def _(s):
        @pl.when(offs[0, 0, s] > strip - size)
        def _():
            one_slot(
                offs[0, 0, s], offs[0, 1, s], obj, acc, probe, d_ref, dt_ref, counts.at[s],
                counts_copy(meas_hbm, counts, sem_meas, s).wait,
                probe_acc, (wave, far, grad, patch, probe_low),
            )

    mine = lax.rem(lax.axis_index(axis), 2)
    blocks, share = keep.shape[:2]
    flat = probe_acc.reshape(2 * blocks * share, size)
    for k in range(blocks):
        keep[k] = flat[pl.ds(pl.multiple_of((2 * k + mine) * share, share), share), :]
        send[k] = flat[pl.ds(pl.multiple_of((2 * k + 1 - mine) * share, share), share), :].astype(
            jnp.bfloat16
        )


def round_kernel(acc, edge_top, edge_low):
    half = edge_top.shape[1]
    start = acc.shape[2] - 2 * half
    for j in range(acc.shape[1]):
        cols = slice(j * LANES, (j + 1) * LANES)
        edge_top[:, :, cols] = acc[:, j, start : start + half, :].astype(jnp.bfloat16)
        edge_low[:, :, cols] = acc[:, j, start + half :, :].astype(jnp.bfloat16)


def split_kernel(axis, bit, value, got, keep, send):
    mine = lax.rem(lax.axis_index(axis) // bit, 2)
    keep[...] = value[:, mine] + got[:, mine].astype(jnp.float32)
    send[...] = (value[:, 1 - mine] + got[:, 1 - mine].astype(jnp.float32)).astype(jnp.bfloat16)


def lower_kernel(acc, grad_hbm, sem):
    strip = grad_hbm.shape[1]
    start = acc.shape[2] - strip
    copies = [
        pltpu.make_async_copy(
            acc.at[:, j, pl.ds(start, strip - start), :],
            grad_hbm.at[:, pl.ds(start, strip - start), pl.ds(j * LANES, LANES)],
            sem,
        )
        for j in range(acc.shape[1])
    ]
    for c in copies:
        c.start()
    for c in copies:
        c.wait()


def add_edge(at, acc, edge, grad_hbm, stage, sem):
    rows = edge.shape[1]
    copies = []
    for j in range(acc.shape[1]):
        stage[:, j, :, :] = acc[:, j, at : at + rows, :] + edge[
            :, :, j * LANES : (j + 1) * LANES
        ].astype(jnp.float32)
        copies += [
            pltpu.make_async_copy(
                stage.at[:, j], grad_hbm.at[:, pl.ds(at, rows), pl.ds(j * LANES, LANES)], sem
            )
        ]
        copies[-1].start()
    return copies


def top_kernel(grad_in, acc, edge, grad_hbm, stage, sem):
    del grad_in
    for c in add_edge(0, acc, edge, grad_hbm, stage, sem):
        c.wait()


def final_kernel(grad_in, acc, edge, mine, other, grad_hbm, probe_hbm, stage, total, sem, sem_probe):
    del grad_in
    total[...] = mine[...] + other[...].astype(jnp.float32)
    whole = pltpu.make_async_copy(total, probe_hbm, sem_probe)
    whole.start()
    for c in add_edge(edge.shape[1], acc, edge, grad_hbm, stage, sem):
        c.wait()
    whole.wait()


def reduce_and_pass_edges(keep, send, edges, axis, params):
    vmem = pl.BlockSpec(memory_space=pltpu.VMEM)
    devices = lax.axis_size(axis)
    blocks, share, lanes = keep.shape
    arrived = []
    bit = 1
    while True:
        stage = bit.bit_length() - 1
        if stage in (1, 2):
            edge = edges[stage - 1]
            edge, send = lax.optimization_barrier((edge, send))
            arrived.append(shifted(edge, axis, 1))
        got = lax.ppermute(send, axis, [(s, s ^ bit) for s in range(devices)])
        bit *= 2
        if bit >= devices:
            return keep, got, arrived
        blocks //= 2
        shape = (blocks, 2, share, lanes)
        keep, send = pl.pallas_call(
            functools.partial(split_kernel, axis, bit),
            out_shape=(
                jax.ShapeDtypeStruct((blocks, share, lanes), jnp.float32),
                jax.ShapeDtypeStruct((blocks, share, lanes), jnp.bfloat16),
            ),
            in_specs=[vmem, vmem],
            out_specs=(vmem, vmem),
            compiler_params=params,
            name="split",
        )(keep.reshape(shape), got.reshape(shape))


def gradients(object_field, probe_modes, scan_offsets, scan_counts, measured):
    size = probe_modes.shape[-1]
    modes = probe_modes.shape[0]
    strip, cols = object_field.shape[1:]
    slots = measured.shape[1]
    blocks = cols // LANES
    scan_offsets = jnp.swapaxes(scan_offsets, 1, 2)
    table, table_t = dft_tables(size)
    d_mat = jnp.asarray(table)
    dt_mat = jnp.asarray(table_t)
    probe = probe_modes.reshape(2 * modes, size, size)
    halo = shifted(object_field[:, :size, :].astype(jnp.bfloat16), "tr", -1)

    f32 = jnp.float32
    bf16 = jnp.bfloat16
    vmem = pl.BlockSpec(memory_space=pltpu.VMEM)
    smem = pl.BlockSpec(memory_space=pltpu.SMEM)
    hbm = pl.BlockSpec(memory_space=pltpu.HBM)
    work = [
        pltpu.VMEM((slots, size, size), jnp.int32),
        pltpu.VMEM((modes * size, 2 * size), bf16),
        pltpu.VMEM((2 * size, modes * size), f32),
        pltpu.VMEM((2 * size, modes * size), bf16),
        pltpu.VMEM((2, size, size), bf16),
    ]
    params = pltpu.CompilerParams(vmem_limit_bytes=16 * 1024 * 1024)
    cost = pl.CostEstimate(
        flops=16 * modes * size * size * size * 4 * slots // 2, bytes_accessed=8 << 20, transcendentals=0
    )
    in_hbm = lambda x: pltpu.with_memory_space_constraint(x, pltpu.HBM)
    probe, d_mat, dt_mat = in_hbm(probe), in_hbm(d_mat), in_hbm(dt_mat)
    object_hbm, measured = in_hbm(object_field), in_hbm(measured)
    tall = jax.ShapeDtypeStruct((2, blocks, strip + size, LANES), f32)
    planes = jax.ShapeDtypeStruct((2 * modes, size, size), f32)
    low_planes = jax.ShapeDtypeStruct(planes.shape, bf16)
    square = jax.ShapeDtypeStruct((2 * size, 2 * size), bf16)
    obj, acc, probe_acc, probe, d_mat, dt_mat, probe_low = pl.pallas_call(
        inner_kernel,
        out_shape=(tall, tall, planes, planes, square, square, low_planes),
        in_specs=[smem, smem, hbm, hbm, hbm, hbm, hbm],
        out_specs=(vmem,) * 7,
        scratch_shapes=work + [pltpu.SemaphoreType.DMA, pltpu.SemaphoreType.DMA((slots,))],
        compiler_params=params,
        cost_estimate=cost,
        name="inner",
    )(scan_offsets, scan_counts, object_hbm, probe, d_mat, dt_mat, measured)
    devices = lax.axis_size("tr")
    shares = (devices // 2, 2 * modes * size // devices, size)
    _, acc, keep, send, _ = pl.pallas_call(
        functools.partial(edge_kernel, "tr"),
        out_shape=(
            tall,
            tall,
            jax.ShapeDtypeStruct(shares, f32),
            jax.ShapeDtypeStruct(shares, bf16),
            planes,
        ),
        in_specs=[smem, smem] + [vmem] * 8 + [hbm],
        out_specs=(vmem,) * 5,
        scratch_shapes=work + [pltpu.SemaphoreType.DMA((slots,))],
        input_output_aliases={3: 0, 4: 1, 5: 4},
        compiler_params=params,
        cost_estimate=cost,
        name="edge",
    )(scan_offsets, scan_counts, halo, obj, acc, probe_acc, probe, probe_low, d_mat, dt_mat, measured)
    small = pltpu.CompilerParams(vmem_limit_bytes=8 * 1024 * 1024)
    edge_top, edge_low = pl.pallas_call(
        round_kernel,
        out_shape=(jax.ShapeDtypeStruct((2, size // 2, cols), bf16),) * 2,
        in_specs=[vmem],
        out_specs=(vmem,) * 2,
        compiler_params=small,
        cost_estimate=pl.CostEstimate(flops=1 << 19, bytes_accessed=3 << 20, transcendentals=0),
        name="rounding",
    )(acc)
    own, other, edges = reduce_and_pass_edges(keep, send, (edge_top, edge_low), "tr", small)
    grad = pl.pallas_call(
        lower_kernel,
        out_shape=jax.ShapeDtypeStruct(object_field.shape, f32),
        in_specs=[vmem],
        out_specs=hbm,
        scratch_shapes=[pltpu.SemaphoreType.DMA],
        compiler_params=small,
        name="lower",
    )(acc)
    scratch = [pltpu.VMEM((2, blocks, size // 2, LANES), f32), pltpu.SemaphoreType.DMA]
    grad = pl.pallas_call(
        top_kernel,
        out_shape=jax.ShapeDtypeStruct(object_field.shape, f32),
        in_specs=[hbm, vmem, vmem],
        out_specs=hbm,
        scratch_shapes=scratch,
        input_output_aliases={0: 0},
        compiler_params=small,
        name="top",
    )(grad, acc, edges[0])
    return pl.pallas_call(
        final_kernel,
        out_shape=(
            jax.ShapeDtypeStruct(object_field.shape, f32),
            jax.ShapeDtypeStruct(own.shape[1:], f32),
        ),
        in_specs=[hbm, vmem, vmem, vmem, vmem],
        out_specs=(hbm, hbm),
        scratch_shapes=scratch[:1]
        + [pltpu.VMEM(own.shape[1:], f32), scratch[1], pltpu.SemaphoreType.DMA],
        input_output_aliases={0: 0},
        compiler_params=small,
        name="finish",
    )(grad, acc, edges[1], own[0], other[0])


def solution(mesh):
    return jax.shard_map(
        gradients,
        mesh=mesh,
        in_specs=(
            P(None, ("groups", "tr"), None),
            P(),
            P(("groups", "tr"), None, None),
            P(("groups", "tr")),
            P(("groups", "tr"), None, None, None),
        ),
        out_specs=(P(None, ("groups", "tr"), None), P(("groups", "tr"), None)),
        check_vma=False,
    )
```

```python
import functools

import jax
import jax.numpy as jnp
import ml_dtypes
import numpy as np
from jax import lax
from jax.experimental import pallas as pl
from jax.experimental.pallas import tpu as pltpu
from jax.sharding import PartitionSpec as P

loss_scale = 1.0 / 1024.0
LANES = 128


def shifted(value, axis, steps):
    count = lax.axis_size(axis)
    initial, last = (max(0, -steps), min(count, count - steps))
    return lax.ppermute(value, axis, [(source, source + steps) for source in range(initial, last)])


def dft_tables(size):
    index = np.arange(size)
    angle = -2.0 * np.pi / size * (index[:, None] * index[None, :] % size)
    scale = 1.0 / np.sqrt(size)
    real = np.cos(angle) * scale
    imag = np.sin(angle) * scale
    table = np.block([[real, imag], [-imag, real]]).astype(np.float32)
    table = table.astype(ml_dtypes.bfloat16)
    return table, np.ascontiguousarray(table.T)


def one_slot(row, col, obj, acc, probe, d_ref, dt_ref, counts, wait_counts, probe_acc, work):
    wave, far, grad, patch, probe_low = work
    size = probe.shape[-1]
    modes = probe.shape[0] // 2
    blocks = size // LANES
    chunk = 64
    first = jnp.minimum(col // LANES, obj.shape[1] - blocks - 1)
    shift = col - first * LANES
    lane = lax.broadcasted_iota(jnp.int32, (chunk, LANES), 1)
    back_by = lax.rem(LANES - shift, LANES)
    for lo in range(0, size, chunk):
        rows = pl.ds(lo, chunk)
        parts = []
        for plane in range(2):
            rolled = [
                pltpu.roll(obj[plane, first + j, pl.ds(row + lo, chunk), :], back_by, 1)
                for j in range(blocks + 1)
            ]
            part = jnp.concatenate(
                [
                    jnp.where(lane < LANES - shift, rolled[j], rolled[j + 1])
                    for j in range(blocks)
                ],
                axis=1,
            )
            patch[plane, rows, :] = part.astype(jnp.bfloat16)
            parts.append(part)
        o_re, o_im = parts
        for m in range(modes):
            p_re = probe[2 * m, rows, :]
            p_im = probe[2 * m + 1, rows, :]
            wave[pl.ds(m * size + lo, chunk), :size] = (p_re * o_re - p_im * o_im).astype(
                jnp.bfloat16
            )
            wave[pl.ds(m * size + lo, chunk), size:] = (p_re * o_im + p_im * o_re).astype(
                jnp.bfloat16
            )
    for part in range(2):
        half = jnp.dot(
            wave[...], d_ref[:, part * size : (part + 1) * size], preferred_element_type=jnp.float32
        ).astype(jnp.bfloat16)
        for m in range(modes):
            grad[part * size : (part + 1) * size, m * size : (m + 1) * size] = half[
                m * size : (m + 1) * size
            ]
    for m in range(modes):
        far[:, m * size : (m + 1) * size] = jnp.dot(
            dt_ref[...], grad[:, m * size : (m + 1) * size], preferred_element_type=jnp.float32
        )
    wait_counts()
    step = 16
    for lo in range(0, size, step):
        re = [far[pl.ds(lo, step), m * size : (m + 1) * size] for m in range(modes)]
        im = [far[pl.ds(size + lo, step), m * size : (m + 1) * size] for m in range(modes)]
        power = 1.0
        for m in range(modes):
            power = power + (re[m] * re[m] + im[m] * im[m])
        count = counts[pl.ds(lo, step), :].astype(jnp.float32)
        ratio = count * lax.rsqrt(jnp.maximum(count, 1.0) * power)
        factor = 2.0 * loss_scale - (2.0 * loss_scale) * ratio
        for m in range(modes):
            grad[pl.ds(lo, step), m * size : (m + 1) * size] = (re[m] * factor).astype(jnp.bfloat16)
            grad[pl.ds(size + lo, step), m * size : (m + 1) * size] = (im[m] * factor).astype(
                jnp.bfloat16
            )
    for m in range(modes):
        back = jnp.dot(
            d_ref[...], grad[:, m * size : (m + 1) * size], preferred_element_type=jnp.float32
        ).astype(jnp.bfloat16)
        for part in range(2):
            wave[m * size : (m + 1) * size, part * size : (part + 1) * size] = back[
                part * size : (part + 1) * size
            ]
    for part in range(2):
        grad[:, part * size : (part + 1) * size] = jnp.dot(
            wave[...], dt_ref[:, part * size : (part + 1) * size], preferred_element_type=jnp.float32
        ).astype(jnp.bfloat16)
    step = 32
    lane = lax.broadcasted_iota(jnp.int32, (step, LANES), 1)
    forth_by = lax.rem(shift, LANES)
    for lo in range(0, size, step):
        rows = pl.ds(lo, step)
        sums = None
        o_re = patch[0, rows, :]
        o_im = patch[1, rows, :]
        for m in range(modes):
            g_re = grad[pl.ds(m * size + lo, step), :size]
            g_im = grad[pl.ds(m * size + lo, step), size:]
            p_re = probe_low[2 * m, rows, :]
            p_im = probe_low[2 * m + 1, rows, :]
            probe_acc[2 * m, rows, :] += (o_re * g_re + o_im * g_im).astype(jnp.float32)
            probe_acc[2 * m + 1, rows, :] += (o_re * g_im - o_im * g_re).astype(jnp.float32)
            term = (p_re * g_re + p_im * g_im, p_re * g_im - p_im * g_re)
            sums = term if sums is None else (sums[0] + term[0], sums[1] + term[1])
        for plane in range(2):
            rolled = [
                pltpu.roll(
                sums[plane][:, j * LANES : (j + 1) * LANES].astype(jnp.float32), forth_by, 1
            )
                for j in range(blocks)
            ]
            for j in range(blocks + 1):
                left = rolled[j - 1] if j > 0 else 0.0
                right = rolled[j] if j < blocks else 0.0
                acc[plane, first + j, pl.ds(row + lo, step), :] += jnp.where(
                    lane >= shift, right, left
                )


def counts_copy(meas_hbm, counts, sem, s):
    return pltpu.make_async_copy(meas_hbm.at[0, s], counts.at[s], sem.at[s])


def inner_kernel(
    offs, cnt, obj_hbm, probe_hbm, d_hbm, dt_hbm, meas_hbm,
    obj, acc, probe_acc, probe, d_ref, dt_ref, probe_low,
    counts, wave, far, grad, patch, sem_obj, sem_meas,
):
    size = probe.shape[-1]
    strip = obj_hbm.shape[1]
    slots = meas_hbm.shape[1]
    copies = [
        pltpu.make_async_copy(
            obj_hbm.at[:, :, pl.ds(j * LANES, LANES)], obj.at[:, j, pl.ds(0, strip), :], sem_obj
        )
        for j in range(obj.shape[1])
    ]
    copies += [
        pltpu.make_async_copy(probe_hbm, probe, sem_obj),
        pltpu.make_async_copy(d_hbm, d_ref, sem_obj),
        pltpu.make_async_copy(dt_hbm, dt_ref, sem_obj),
    ]
    for c in copies:
        c.start()
    used = cnt[0]

    for s in range(slots):

        @pl.when(jnp.logical_and(s < used, offs[0, 0, s] <= strip - size))
        def _():
            counts_copy(meas_hbm, counts, sem_meas, s).start()

    acc[...] = jnp.zeros_like(acc)
    probe_acc[...] = jnp.zeros_like(probe_acc)
    for c in copies:
        c.wait()
    probe_low[...] = probe[...].astype(jnp.bfloat16)

    @pl.loop(0, used)
    def _(s):
        @pl.when(offs[0, 0, s] <= strip - size)
        def _():
            one_slot(
                offs[0, 0, s], offs[0, 1, s], obj, acc, probe, d_ref, dt_ref, counts.at[s],
                counts_copy(meas_hbm, counts, sem_meas, s).wait,
                probe_acc, (wave, far, grad, patch, probe_low),
            )


def edge_kernel(
    axis, offs, cnt, halo, obj_in, acc_in, probe_in, probe, probe_low, d_ref, dt_ref, meas_hbm,
    obj, acc, send, probe_acc,
    counts, wave, far, grad, patch, sem_meas,
):
    del obj_in, acc_in, probe_in
    size = probe.shape[-1]
    strip = obj.shape[2] - size
    slots = meas_hbm.shape[1]
    used = cnt[0]

    for s in range(slots):

        @pl.when(jnp.logical_and(s < used, offs[0, 0, s] > strip - size))
        def _():
            counts_copy(meas_hbm, counts, sem_meas, s).start()

    for j in range(obj.shape[1]):
        obj[:, j, strip:, :] = halo[:, :, j * LANES : (j + 1) * LANES].astype(jnp.float32)

    @pl.loop(0, used)
    def _(s):
        @pl.when(offs[0, 0, s] > strip - size)
        def _():
            one_slot(
                offs[0, 0, s], offs[0, 1, s], obj, acc, probe, d_ref, dt_ref, counts.at[s],
                counts_copy(meas_hbm, counts, sem_meas, s).wait,
                probe_acc, (wave, far, grad, patch, probe_low),
            )

    mine = lax.rem(lax.axis_index(axis), 2)
    blocks, share = send.shape[:2]
    flat = probe_acc.reshape(2 * blocks * share, size)
    for k in range(blocks):
        send[k] = flat[pl.ds(pl.multiple_of((2 * k + 1 - mine) * share, share), share), :].astype(
            jnp.bfloat16
        )


def round_kernel(axis, acc, probe_acc, edge_top, edge_low, keep):
    mine = lax.rem(lax.axis_index(axis), 2)
    keep[...] = probe_acc[:, mine]
    half = edge_top.shape[1]
    start = acc.shape[2] - 2 * half
    for j in range(acc.shape[1]):
        cols = slice(j * LANES, (j + 1) * LANES)
        edge_top[:, :, cols] = acc[:, j, start : start + half, :].astype(jnp.bfloat16)
        edge_low[:, :, cols] = acc[:, j, start + half :, :].astype(jnp.bfloat16)


def split_kernel(axis, bit, value, got, keep, send):
    mine = lax.rem(lax.axis_index(axis) // bit, 2)
    keep[...] = value[:, mine] + got[:, mine].astype(jnp.float32)
    send[...] = (value[:, 1 - mine] + got[:, 1 - mine].astype(jnp.float32)).astype(jnp.bfloat16)


def lower_kernel(acc, grad_hbm, sem):
    strip = grad_hbm.shape[1]
    start = acc.shape[2] - strip
    copies = [
        pltpu.make_async_copy(
            acc.at[:, j, pl.ds(start, strip - start), :],
            grad_hbm.at[:, pl.ds(start, strip - start), pl.ds(j * LANES, LANES)],
            sem,
        )
        for j in range(acc.shape[1])
    ]
    for c in copies:
        c.start()
    for c in copies:
        c.wait()


def add_edge(at, acc, edge, grad_hbm, stage, sem):
    rows = edge.shape[1]
    copies = []
    for j in range(acc.shape[1]):
        stage[:, j, :, :] = acc[:, j, at : at + rows, :] + edge[
            :, :, j * LANES : (j + 1) * LANES
        ].astype(jnp.float32)
        copies += [
            pltpu.make_async_copy(
                stage.at[:, j], grad_hbm.at[:, pl.ds(at, rows), pl.ds(j * LANES, LANES)], sem
            )
        ]
        copies[-1].start()
    return copies


def top_kernel(grad_in, acc, edge, grad_hbm, stage, sem):
    del grad_in
    for c in add_edge(0, acc, edge, grad_hbm, stage, sem):
        c.wait()


def final_kernel(grad_in, acc, edge, mine, other, grad_hbm, probe_hbm, stage, total, sem, sem_probe):
    del grad_in
    total[...] = mine[...] + other[...].astype(jnp.float32)
    whole = pltpu.make_async_copy(total, probe_hbm, sem_probe)
    whole.start()
    for c in add_edge(edge.shape[1], acc, edge, grad_hbm, stage, sem):
        c.wait()
    whole.wait()


def reduce_and_pass_edges(keep, send, edges, axis, params):
    vmem = pl.BlockSpec(memory_space=pltpu.VMEM)
    devices = lax.axis_size(axis)
    blocks, share, lanes = keep.shape
    arrived = []
    bit = 1
    while True:
        stage = bit.bit_length() - 1
        if stage in (1, 2):
            edge = edges[stage - 1]
            edge, send = lax.optimization_barrier((edge, send))
            arrived.append(shifted(edge, axis, 1))
        got = lax.ppermute(send, axis, [(s, s ^ bit) for s in range(devices)])
        bit *= 2
        if bit >= devices:
            return keep, got, arrived
        blocks //= 2
        shape = (blocks, 2, share, lanes)
        keep, send = pl.pallas_call(
            functools.partial(split_kernel, axis, bit),
            out_shape=(
                jax.ShapeDtypeStruct((blocks, share, lanes), jnp.float32),
                jax.ShapeDtypeStruct((blocks, share, lanes), jnp.bfloat16),
            ),
            in_specs=[vmem, vmem],
            out_specs=(vmem, vmem),
            compiler_params=params,
            name="split",
        )(keep.reshape(shape), got.reshape(shape))


def gradients(object_field, probe_modes, scan_offsets, scan_counts, measured):
    size = probe_modes.shape[-1]
    modes = probe_modes.shape[0]
    strip, cols = object_field.shape[1:]
    slots = measured.shape[1]
    blocks = cols // LANES
    scan_offsets = jnp.swapaxes(scan_offsets, 1, 2)
    table, table_t = dft_tables(size)
    d_mat = jnp.asarray(table)
    dt_mat = jnp.asarray(table_t)
    probe = probe_modes.reshape(2 * modes, size, size)
    halo = shifted(object_field[:, :size, :].astype(jnp.bfloat16), "tr", -1)

    f32 = jnp.float32
    bf16 = jnp.bfloat16
    vmem = pl.BlockSpec(memory_space=pltpu.VMEM)
    smem = pl.BlockSpec(memory_space=pltpu.SMEM)
    hbm = pl.BlockSpec(memory_space=pltpu.HBM)
    work = [
        pltpu.VMEM((slots, size, size), jnp.int32),
        pltpu.VMEM((modes * size, 2 * size), bf16),
        pltpu.VMEM((2 * size, modes * size), f32),
        pltpu.VMEM((2 * size, modes * size), bf16),
        pltpu.VMEM((2, size, size), bf16),
    ]
    params = pltpu.CompilerParams(vmem_limit_bytes=16 * 1024 * 1024)
    cost = pl.CostEstimate(
        flops=16 * modes * size * size * size * 4 * slots // 2, bytes_accessed=8 << 20, transcendentals=0
    )
    in_hbm = lambda x: pltpu.with_memory_space_constraint(x, pltpu.HBM)
    probe, d_mat, dt_mat = in_hbm(probe), in_hbm(d_mat), in_hbm(dt_mat)
    object_hbm, measured = in_hbm(object_field), in_hbm(measured)
    tall = jax.ShapeDtypeStruct((2, blocks, strip + size, LANES), f32)
    planes = jax.ShapeDtypeStruct((2 * modes, size, size), f32)
    low_planes = jax.ShapeDtypeStruct(planes.shape, bf16)
    square = jax.ShapeDtypeStruct((2 * size, 2 * size), bf16)
    obj, acc, probe_acc, probe, d_mat, dt_mat, probe_low = pl.pallas_call(
        inner_kernel,
        out_shape=(tall, tall, planes, planes, square, square, low_planes),
        in_specs=[smem, smem, hbm, hbm, hbm, hbm, hbm],
        out_specs=(vmem,) * 7,
        scratch_shapes=work + [pltpu.SemaphoreType.DMA, pltpu.SemaphoreType.DMA((slots,))],
        compiler_params=params,
        cost_estimate=cost,
        name="inner",
    )(scan_offsets, scan_counts, object_hbm, probe, d_mat, dt_mat, measured)
    devices = lax.axis_size("tr")
    shares = (devices // 2, 2 * modes * size // devices, size)
    _, acc, send, probe_acc = pl.pallas_call(
        functools.partial(edge_kernel, "tr"),
        out_shape=(
            tall,
            tall,
            jax.ShapeDtypeStruct(shares, bf16),
            planes,
        ),
        in_specs=[smem, smem] + [vmem] * 8 + [hbm],
        out_specs=(vmem,) * 4,
        scratch_shapes=work + [pltpu.SemaphoreType.DMA((slots,))],
        input_output_aliases={3: 0, 4: 1, 5: 3},
        compiler_params=params,
        cost_estimate=cost,
        name="edge",
    )(scan_offsets, scan_counts, halo, obj, acc, probe_acc, probe, probe_low, d_mat, dt_mat, measured)
    small = pltpu.CompilerParams(vmem_limit_bytes=8 * 1024 * 1024)
    edge_top, edge_low, keep = pl.pallas_call(
        functools.partial(round_kernel, "tr"),
        out_shape=(jax.ShapeDtypeStruct((2, size // 2, cols), bf16),) * 2
        + (jax.ShapeDtypeStruct(shares, f32),),
        in_specs=[vmem] * 2,
        out_specs=(vmem,) * 3,
        compiler_params=small,
        cost_estimate=pl.CostEstimate(flops=1 << 19, bytes_accessed=3 << 20, transcendentals=0),
        name="rounding",
    )(acc, probe_acc.reshape(shares[0], 2, *shares[1:]))
    own, other, edges = reduce_and_pass_edges(keep, send, (edge_top, edge_low), "tr", small)
    grad = pl.pallas_call(
        lower_kernel,
        out_shape=jax.ShapeDtypeStruct(object_field.shape, f32),
        in_specs=[vmem],
        out_specs=hbm,
        scratch_shapes=[pltpu.SemaphoreType.DMA],
        compiler_params=small,
        name="lower",
    )(acc)
    scratch = [pltpu.VMEM((2, blocks, size // 2, LANES), f32), pltpu.SemaphoreType.DMA]
    grad = pl.pallas_call(
        top_kernel,
        out_shape=jax.ShapeDtypeStruct(object_field.shape, f32),
        in_specs=[hbm, vmem, vmem],
        out_specs=hbm,
        scratch_shapes=scratch,
        input_output_aliases={0: 0},
        compiler_params=small,
        name="top",
    )(grad, acc, edges[0])
    return pl.pallas_call(
        final_kernel,
        out_shape=(
            jax.ShapeDtypeStruct(object_field.shape, f32),
            jax.ShapeDtypeStruct(own.shape[1:], f32),
        ),
        in_specs=[hbm, vmem, vmem, vmem, vmem],
        out_specs=(hbm, hbm),
        scratch_shapes=scratch[:1]
        + [pltpu.VMEM(own.shape[1:], f32), scratch[1], pltpu.SemaphoreType.DMA],
        input_output_aliases={0: 0},
        compiler_params=small,
        name="finish",
    )(grad, acc, edges[1], own[0], other[0])


def solution(mesh):
    return jax.shard_map(
        gradients,
        mesh=mesh,
        in_specs=(
            P(None, ("groups", "tr"), None),
            P(),
            P(("groups", "tr"), None, None),
            P(("groups", "tr")),
            P(("groups", "tr"), None, None, None),
        ),
        out_specs=(P(None, ("groups", "tr"), None), P(("groups", "tr"), None)),
        check_vma=False,
    )
```
